32 devices in a mesh: group: 2 (over y), blk: 4 (over z), gz: 2 (over x), view: 2 (over core).
Axes of the slice: x: 2, y: 2, z: 4, core: 2. Of those that a mesh axis runs over, the one named last changes fastest.
Arguments:
- estimate: float32 [32, 128, 128], P(('group', 'gz'), 'blk'), parts along dimension 0, may hold values from 0.5 to 2
- view_tiles: bfloat16 [192, 14, 14, 128], P(('group', 'blk', 'gz', 'view')), parts along dimension 0, may hold values from 0.25 to 4
- tile_pairs: int32 [192, 2], P('group'), parts along dimension 0, may hold values from 0 to 31, as said below
- kernel_table: bfloat16 [6, 16, 7, 7, 7], P('view', ('group', 'blk', 'gz')), parts along dimension 1, may hold values from 0.0014953613 to 0.0059814453
- kernel_ids: int32 [64, 6], P('group'), parts along dimension 0, may hold values from 0 to 7
Outputs:
- estimate_out: float32 [32, 128, 128], P(('group', 'gz'), 'blk'), parts along dimension 0
The draws below stay inside these ranges and needn't reach their ends.
There are 2 independent parts, one for each index of `group`. The reference program is written for one: setup_inputs(seed, part) draws one part's arguments, and reference() takes and returns one part's arrays. A program takes and returns all parts, laid end to end along the dimension named above; each array names one. Nothing has to cross between parts.
Inputs may be any that keep to these rules, and one draw needn't show every extreme that they name: Tile t is stored on the device at position t // 6 in the order blk, gz, view. Its block b = tile_pairs[t, 0] lies in that device's sub-slab (b // 16 is its gz index) and its view tile_pairs[t, 1] in that device's half (view // 3 is its view index). No block has two tiles of one view; every block has at least one tile of each half of the views. The tiles of one device go to at most 3 tiles' worth of blocks with the same (b % 16) // 4, and some device reaches 3; the blocks of one sub-slab with the same (b % 16) // 4 have at most 12 tiles of one half of the views, and some reach it.
All inputs are finite; a program needn't handle non-finite values.
Results may differ from the reference program's by a relative error of at most 0.0003.
Values may be sent and summed in bfloat16 or wider, within the bound.
No kernel may reach another device: no remote copies, remote signals or barrier semaphores. Data moves between devices by JAX's collectives and lax.ppermute only.
A program may use at most 64 MiB of HBM per device.

```python
import math
from functools import partial
import jax
import jax.numpy as jnp
from jax import lax

CZ = 8
BY = 8
NX = 128
BLK_DEV = 4
VIEWS = 6
R = 3
ITERS = 2
K = 7
TILE_DEV = 6
NBY = 16
NZ = 16
NY = 128
NBLOCKS = 32
NTILES = 96
NPSFV = 8
EZ = 14
EY = 14
N_BLK = 4
N_GZ = 2
N_VIEW = 2


def shuffle_pairs(subkey, pair_count):
    return jax.random.permutation(subkey, pair_count)


def group_tables(base_key, group):
    views_core = VIEWS // N_VIEW
    home_count = N_BLK
    most_home = views_core * BLK_DEV
    entry_count = home_count * TILE_DEV
    spare_load = home_count * (TILE_DEV - BLK_DEV)
    group_key = jax.random.fold_in(base_key, group)
    subkeys = jax.random.split(group_key, 5)
    home_order = jax.random.permutation(subkeys[0], home_count)
    source_order = jax.random.permutation(subkeys[1], home_count)
    ceiling = (views_core - 1) * BLK_DEV
    limits = jax.random.randint(subkeys[2], (home_count,), ceiling // 2, ceiling + 1)
    limits = limits.at[0].set(ceiling)
    before = jnp.cumsum(limits) - limits
    extra_load = jnp.clip(spare_load - before, 0, limits)
    home_loads = BLK_DEV + extra_load
    load_ends = jnp.cumsum(home_loads)
    entry_ids = jnp.arange(entry_count, dtype=jnp.int32)
    placed = jnp.sum((load_ends[None, :] <= entry_ids[:, None]).astype(jnp.int32), axis=1)
    within = entry_ids - (load_ends - home_loads)[placed]
    home_ids = home_order[placed]
    source_ids = source_order[entry_ids % home_count]
    slot_ids = entry_ids // home_count
    first_views = jax.random.randint(subkeys[3], (home_count, BLK_DEV), 0, views_core)
    pair_ids = jnp.arange(most_home, dtype=jnp.int32)
    pair_block = pair_ids // views_core
    pair_view = pair_ids % views_core
    shuffles = jax.vmap(partial(shuffle_pairs, pair_count=most_home))(jax.random.split(subkeys[4], home_count))
    leading = pair_view[None, :] == first_views[:, pair_block]
    scores = jnp.where(leading, pair_block[None, :], most_home + shuffles)
    ordered = jnp.argsort(scores, axis=1)
    chosen = ordered[home_ids, within]
    slab_index = group // N_VIEW
    core_index = group % N_VIEW
    block_ids = slab_index * BLK_DEV * N_BLK + home_ids * BLK_DEV + chosen // views_core
    view_ids = core_index * views_core + chosen % views_core
    devices = source_ids * (N_GZ * N_VIEW) + slab_index * N_VIEW + core_index
    positions = devices * TILE_DEV + slot_ids
    return (positions, block_ids, view_ids)


def draw_tile_pairs(key, part):
    base_key = jax.random.fold_in(key, 7301)
    positions, block_ids, view_ids = jax.vmap(partial(group_tables, base_key))(jnp.arange(N_GZ * N_VIEW, dtype=jnp.int32))
    positions = positions.reshape(-1)
    block_table = jnp.zeros((NTILES,), jnp.int32).at[positions].set(block_ids.reshape(-1).astype(jnp.int32))
    view_table = jnp.zeros((NTILES,), jnp.int32).at[positions].set(view_ids.reshape(-1).astype(jnp.int32))
    return jnp.stack([block_table, view_table], axis=1).astype(jnp.int32)


def touch_ends(entries, stream_key, smallest, largest):
    shape = entries.shape
    index_at = [jax.random.randint(jax.random.fold_in(stream_key, axis), (), 0, shape[axis]) for axis in range(len(shape))]
    entries = entries.at[tuple(index_at)].set(smallest)
    longest = shape.index(max(shape))
    index_at[longest] = (index_at[longest] + 1) % shape[longest]
    return entries.at[tuple(index_at)].set(largest)


def level_of(key, dims, pieces, least, largest):
    level = 1.0
    for axis_at, blocks in pieces:
        draws = jax.random.uniform(jax.random.fold_in(jax.random.fold_in(key, 6), axis_at), (blocks,), jnp.float32, least / len(pieces), largest / len(pieces))
        level = level * jnp.repeat(jnp.exp(draws), dims[axis_at] // blocks).reshape((-1,) + (1,) * (len(dims) - 1 - axis_at))
    return level


def setup_inputs(seed: int = 0, part: int = 0) -> dict:
    key_list = jax.random.split(jax.random.key(seed), 6)
    own_keys = jax.random.split(jax.random.fold_in(key_list[5], part), 6)
    return {
        "estimate": jnp.clip(jnp.exp(math.log(2.0) - 1.3862944 * jax.random.uniform(own_keys[0], (NZ, NY, NX), jnp.float32) ** level_of(own_keys[0], (NZ, NY, NX), ((0, 2), (1, 4)), -0.2, 0.2)), 0.5, 2.0),
        "view_tiles": jnp.clip(jnp.exp(math.log(4.0) - 2.7725887 * jax.random.uniform(own_keys[1], (NTILES, EZ, EY, NX), jnp.float32) ** level_of(own_keys[1], (NTILES, EZ, EY, NX), ((0, 16),), -0.2, 0.2)), 0.25, 4.0).astype(jnp.bfloat16),
        "tile_pairs": draw_tile_pairs(jax.random.fold_in(jax.random.fold_in(key_list[5], part), 71), part),
        "kernel_table": jnp.clip(jnp.exp(math.log(0.0059814453) - 1.3862944 * jax.random.uniform(own_keys[3], (VIEWS, NPSFV, K, K, K), jnp.float32) ** level_of(own_keys[3], (VIEWS, NPSFV, K, K, K), ((0, 2), (1, 8)), -0.2, 0.2)), 0.0014953613, 0.0059814453).astype(jnp.bfloat16),
        "kernel_ids": touch_ends(jax.random.randint(own_keys[4], (NBLOCKS, VIEWS), 0, NPSFV), jax.random.fold_in(own_keys[4], 1), 0, NPSFV - 1).astype(jnp.int32),
    }


def toeplitz_pair(kernel, cells_x):
    kernel_size = kernel.shape[0]
    kernel_reach = (kernel_size - 1) // 2
    row_index = jnp.arange(cells_x, dtype=jnp.int32)[:, None]
    column_index = jnp.arange(cells_x, dtype=jnp.int32)[None, :]
    tap_index = jnp.arange(kernel_size, dtype=jnp.int32)[:, None, None]
    forward_mask = ((row_index - column_index + kernel_reach)[None] == tap_index).astype(jnp.float32)
    backward_mask = ((column_index - row_index + kernel_reach)[None] == tap_index).astype(jnp.float32)
    kernel_wide = kernel.astype(jnp.float32)
    forward = jnp.einsum("abc,cji->abji", kernel_wide, forward_mask).astype(jnp.bfloat16)
    backward = jnp.einsum("abc,cji->abji", kernel_wide, backward_mask).astype(jnp.bfloat16)
    return (forward.reshape(kernel_size, kernel_size * cells_x, cells_x),
            backward.reshape(kernel_size, kernel_size * cells_x, cells_x))


def blurring(extended, forward, extent_z, extent_y):
    kernel_size = forward.shape[0]
    cells_x = extended.shape[2]
    shifted = jnp.stack([extended[:, shift_y:shift_y + extent_y, :] for shift_y in range(kernel_size)], axis=2)
    shifted = shifted.reshape(extended.shape[0], extent_y, kernel_size * cells_x)
    accumulated = jnp.zeros((extent_z * extent_y, cells_x), jnp.float32)
    for plane_z in range(kernel_size):
        matrix_rows = shifted[plane_z:plane_z + extent_z].reshape(extent_z * extent_y, kernel_size * cells_x)
        accumulated = accumulated + jnp.dot(matrix_rows, forward[plane_z], preferred_element_type=jnp.float32)
    return accumulated.reshape(extent_z, extent_y, cells_x)


def spread(ratio, backward, extent_z, extent_y):
    kernel_size = backward.shape[0]
    kernel_reach = (kernel_size - 1) // 2
    cells_x = ratio.shape[2]
    shifted = jnp.stack([ratio[:, 2 * kernel_reach - shift_y:2 * kernel_reach - shift_y + extent_y, :]
                         for shift_y in range(kernel_size)], axis=2)
    shifted = shifted.reshape(ratio.shape[0], extent_y, kernel_size * cells_x)
    accumulated = jnp.zeros((extent_z * extent_y, cells_x), jnp.float32)
    for plane_z in range(kernel_size):
        begin_z = 2 * kernel_reach - plane_z
        matrix_rows = shifted[begin_z:begin_z + extent_z].reshape(extent_z * extent_y, kernel_size * cells_x)
        accumulated = accumulated + jnp.dot(matrix_rows, backward[plane_z], preferred_element_type=jnp.float32)
    return accumulated.reshape(extent_z, extent_y, cells_x)


def tile_correction(one_tile, extended, kernel, first_z, first_y, volume_z, volume_y):
    extent_z, extent_y, cells_x = one_tile.shape
    kernel_reach = (kernel.shape[0] - 1) // 2
    forward, backward = toeplitz_pair(kernel, cells_x)
    blurred = blurring(extended, forward, extent_z, extent_y)
    cell_z = first_z + jnp.arange(extent_z, dtype=jnp.int32) - kernel_reach
    cell_y = first_y + jnp.arange(extent_y, dtype=jnp.int32) - kernel_reach
    inside = (((cell_z >= 0) & (cell_z < volume_z))[:, None, None]
              & ((cell_y >= 0) & (cell_y < volume_y))[None, :, None])
    ratio = jnp.where(inside, one_tile.astype(jnp.float32) / blurred, 0.0).astype(jnp.bfloat16)
    return spread(ratio, backward, extent_z - 2 * kernel_reach, extent_y - 2 * kernel_reach)


def reference(estimate, view_tiles, tile_pairs, kernel_table, kernel_ids):
    tile_block = tile_pairs[:, 0]
    tile_view = tile_pairs[:, 1]
    counts = jnp.zeros((NBLOCKS,), jnp.float32).at[tile_block].add(1.0)
    count_field = jnp.repeat(jnp.repeat(counts.reshape(N_GZ, NBY), CZ, axis=0), BY, axis=1)[:, :, None]
    current = estimate
    for iteration in range(ITERS):
        padded = jnp.pad(current.astype(jnp.bfloat16), ((2 * R, 2 * R), (2 * R, 2 * R), (0, 0)))

        def visit_tile(summed, position):
            block_id = tile_block[position]
            view_id = tile_view[position]
            first_z = ((block_id // NBY) * CZ).astype(jnp.int32)
            first_y = ((block_id % NBY) * BY).astype(jnp.int32)
            extended = lax.dynamic_slice(padded, (first_z, first_y, jnp.int32(0)), (CZ + 4 * R, BY + 4 * R, NX))
            kernel = kernel_table[view_id, kernel_ids[block_id, view_id]]
            correction = tile_correction(view_tiles[position], extended, kernel, first_z, first_y, NZ, NY)
            return summed.at[block_id].add(correction), None

        summed, unused = lax.scan(visit_tile, jnp.zeros((NBLOCKS, CZ, BY, NX), jnp.float32),
                                  jnp.arange(NTILES, dtype=jnp.int32))
        field = summed.reshape(N_GZ, NBY, CZ, BY, NX).transpose(0, 2, 1, 3, 4).reshape(NZ, NY, NX)
        current = current * field / count_field
    return current
```

```python
import functools

import jax
import jax.numpy as jnp
from jax import lax
from jax.experimental import pallas as pl
from jax.experimental.pallas import tpu as pltpu
from jax.sharding import PartitionSpec as P

ITERS = 2
F32, BF16 = jnp.float32, jnp.bfloat16
VM = pl.BlockSpec(memory_space=pltpu.VMEM)
SM = pl.BlockSpec(memory_space=pltpu.SMEM)


def up8(n):
    return (n + 7) // 8 * 8


class Plan:
    def __init__(self, estimate, view_tiles, tile_pairs, kernel_table, kernel_ids):
        self.cz, self.ly, self.nx = estimate.shape
        self.tiles, self.ez, self.ey, _ = view_tiles.shape
        self.views_here, self.sets_here, self.taps = kernel_table.shape[:3]
        self.reach = (self.taps - 1) // 2
        self.by = self.ey - 2 * self.reach
        self.blocks = self.ly // self.by
        self.n_blk = lax.axis_size("blk")
        self.n_gz = lax.axis_size("gz")
        self.n_view = lax.axis_size("view")
        self.views = self.views_here * self.n_view
        self.row_blocks = self.blocks * self.n_blk
        self.total = tile_pairs.shape[0]
        self.slots = -(-self.views_here * self.blocks // self.n_blk)
        self.slots = min(self.slots, self.tiles)
        self.fast = self.n_blk == 4 and self.n_gz == 2 and self.sets_here == 1
        self.n_sets = self.n_blk * self.n_gz * self.sets_here
        self.halo = 2 * self.reach
        assert self.by == 8 and self.cz == 8 and self.nx == 128 and self.taps == 7
        assert self.n_blk % 2 == 0 and self.blocks % 2 == 0 and self.ez <= 16
        self.zz = self.cz + 2 * self.halo
        self.rows = self.ly + 16
        self.windows = self.blocks // 2


def ranks():
    return lax.axis_index("blk"), lax.axis_index("gz"), lax.axis_index("view")


def lane_shift(plane, e, reach, lane):
    d = e - reach
    if d == 0:
        return plane
    n = plane.shape[-1]
    rolled = pltpu.roll(plane, (-d) % n, 1)
    ok = (lane < n - d) if d > 0 else (lane >= -d)
    return jnp.where(ok, rolled, 0.0)


def pack_kernel(p, pairs_ref, tiles_ref, *outs):
    b, g, v = ranks()
    first = ((b * p.n_gz + g) * p.n_view + v) * p.tiles
    homes = [(pairs_ref[2 * (first + j)] % p.row_blocks) // p.blocks for j in range(p.tiles)]
    for j in range(p.tiles):
        rank = sum([(homes[i] == homes[j]).astype(jnp.int32) for i in range(j)], jnp.int32(0))
        k = lax.rem(homes[j] - b + p.n_blk, p.n_blk)
        for kk in range(p.n_blk):

            @pl.when(k == kk)
            def _():
                outs[kk][rank] = tiles_ref[j]


def pack(p, pairs, tiles):
    return pl.pallas_call(
        functools.partial(pack_kernel, p),
        out_shape=[jax.ShapeDtypeStruct((p.slots,) + tiles.shape[1:], tiles.dtype)] * p.n_blk,
        in_specs=[SM, VM],
        out_specs=[VM] * p.n_blk,
        name="pack",
    )(pairs, tiles)


def sends_of(p, b, g, x, own_ref, sa_ref, sb_ref):
    even = b % 2 == 0
    for z in range(p.cz):
        xb = x[z].astype(BF16)
        own_ref[z] = xb
        lo, hi = xb[:8], xb[p.ly - 8 :]
        lo, hi = x[z][:8], x[z][p.ly - 8 :]
        sa_ref[z] = jnp.where(even, hi, lo).astype(BF16)
        sb_ref[z] = jnp.where(even, lo, hi).astype(BF16)


def first_kernel(p, est_ref, own_ref, sa_ref, sb_ref):
    b, g, v = ranks()
    sends_of(p, b, g, [est_ref[z] for z in range(p.cz)], own_ref, sa_ref, sb_ref)


def update_kernel(p, count_ref, est_ref, mine_ref, other_ref, new_ref, own_ref=None, sa_ref=None, sb_ref=None):
    b, g, v = ranks()
    x = []
    for z in range(p.cz):
        rows = []
        for k in range(p.blocks):
            at = slice(k * 8, k * 8 + 8)
            total = mine_ref[z, at, :] + other_ref[z, at, :]
            rows.append(est_ref[z, at, :] * total / count_ref[k])
        x.append(jnp.concatenate(rows, axis=0))
        new_ref[z] = x[z]
    if own_ref is not None:
        sends_of(p, b, g, x, own_ref, sa_ref, sb_ref)


def sends_shape(p):
    return [
        jax.ShapeDtypeStruct((p.cz, p.ly, p.nx), BF16),
        jax.ShapeDtypeStruct((p.cz, 8, p.nx), BF16),
        jax.ShapeDtypeStruct((p.cz, 8, p.nx), BF16),
    ]


def first_sends(p, est):
    return pl.pallas_call(
        functools.partial(first_kernel, p), out_shape=sends_shape(p), in_specs=[VM],
        out_specs=[VM] * 3, name="first",
    )(est)


def update(p, count, est, mine, other, last):
    shapes = [jax.ShapeDtypeStruct(est.shape, F32)] + ([] if last else sends_shape(p))
    return pl.pallas_call(
        functools.partial(update_kernel, p), out_shape=shapes, in_specs=[SM, VM, VM, VM],
        out_specs=[VM] * len(shapes), name="update",
    )(count, est, mine, other)


def edges_kernel(p, own_ref, ra_ref, rb_ref, lo_ref, hi_ref=None):
    b, g, v = ranks()
    even = b % 2 == 0
    has_lo, has_hi = b > 0, b < p.n_blk - 1

    def planes(out_ref, start):
        for i in range(p.halo):
            ra, rb = ra_ref[start + i].astype(F32), rb_ref[start + i].astype(F32)
            left = jnp.where(has_lo, jnp.where(even, rb, ra), 0.0)
            right = jnp.where(has_hi, jnp.where(even, ra, rb), 0.0)
            out_ref[i, :8] = left.astype(BF16)
            out_ref[i, 8 : 8 + p.ly] = own_ref[start + i]
            out_ref[i, 8 + p.ly :] = right.astype(BF16)

    if hi_ref is None:
        planes(lo_ref, jnp.where(g == 0, p.cz - p.halo, 0))
    else:
        planes(lo_ref, p.cz - p.halo)
        planes(hi_ref, 0)


def halos(p, own, sa, sb, kern=None):
    n = p.n_blk
    pair = [(i, i ^ 1) for i in range(n)]
    odd = [(i, (i + 1) % n if i % 2 else (i - 1) % n) for i in range(n)]
    nz = p.cz * 8
    if kern is not None and p.fast:
        kr = kern.shape[0]
        got = lax.ppermute(jnp.concatenate([sa.reshape(nz, p.nx), kern]), "blk", pair)
        ra, kern = got[:nz].reshape(sa.shape), jnp.concatenate([kern, got[nz:]])
        got = lax.ppermute(jnp.concatenate([sb.reshape(nz, p.nx), kern]), "blk", odd)
        rb, kern = got[:nz].reshape(sb.shape), jnp.concatenate([kern, got[nz:]])
    else:
        ra, rb = lax.ppermute(sa, "blk", pair), lax.ppermute(sb, "blk", odd)
    two = p.n_gz == 2
    edge = jax.ShapeDtypeStruct((p.halo, p.rows, p.nx), BF16)
    out = pl.pallas_call(
        functools.partial(edges_kernel, p), out_shape=[edge] if two else [edge, edge],
        in_specs=[VM] * 3, out_specs=[VM] * (1 if two else 2), name="edges",
    )(own, ra, rb)
    if two:
        swap = [(0, 1), (1, 0)]
        if kern is not None and p.fast:
            ne = p.halo * p.rows
            got = lax.ppermute(jnp.concatenate([out[0].reshape(ne, p.nx), kern]), "gz", swap)
            below = above = got[:ne].reshape(edge.shape)
            kern = jnp.concatenate([kern, got[ne:]])
        else:
            below = above = lax.ppermute(out[0], "gz", swap)
    else:
        ups = [(i, i + 1) for i in range(p.n_gz - 1)]
        below = lax.ppermute(out[0], "gz", ups)
        above = lax.ppermute(out[1], "gz", [(j, i) for i, j in ups])
    return (own, ra, rb, below, above), kern


def tiles_kernel(p, pairs_ref, ids_ref, own_ref, ra_ref, rb_ref, below_ref, above_ref, kern_ref, *rest):
    arrived = rest[: p.n_blk]
    out_ref, xs_ref, kf_ref, kb_ref, tile_ref, r_ref, r2_ref = rest[p.n_blk :]
    b, g, v = ranks()
    even = b % 2 == 0
    taps, reach, nx = p.taps, p.reach, p.nx
    lane8 = lax.broadcasted_iota(jnp.int32, (8, nx), 1)

    row = lax.broadcasted_iota(jnp.int32, (128, 256), 0)
    col = lax.broadcasted_iota(jnp.int32, (128, 256), 1)
    sel_f = ((row // taps == col % 32) & (row % taps == col // 32) & (row < taps * taps)).astype(BF16)
    row = lax.broadcasted_iota(jnp.int32, (128, 128), 0)
    col = lax.broadcasted_iota(jnp.int32, (128, 128), 1)
    sel_b = (
        (taps - 1 - row // taps == col % 16) & (taps - 1 - row % taps == col // 16) & (row < taps * taps)
    ).astype(BF16)
    kf_ref[...] = jnp.dot(kern_ref[...], sel_f, preferred_element_type=F32)
    kb_ref[...] = jnp.dot(kern_ref[...], sel_b, preferred_element_type=F32)

    depth = taps * 32
    xs_ref[:, depth:, :] = jnp.zeros((p.windows, xs_ref.shape[1] - depth, xs_ref.shape[2]), BF16)
    r2_ref[taps * 16 :, :] = jnp.zeros((r2_ref.shape[0] - taps * 16, r2_ref.shape[1]), BF16)
    r_ref[...] = jnp.zeros(r_ref.shape, F32)
    out_ref[...] = jnp.zeros(out_ref.shape, F32)
    has_left, has_right = b > 0, b < p.n_blk - 1
    has_below, has_above = g > 0, g < p.n_gz - 1
    lane = lax.broadcasted_iota(jnp.int32, (p.rows, nx), 1)
    for z in range(p.zz):
        if z < p.halo:
            plane = jnp.where(has_below, below_ref[z].astype(F32), 0.0)
        elif z >= p.halo + p.cz:
            plane = jnp.where(has_above, above_ref[z - p.halo - p.cz].astype(F32), 0.0)
        else:
            i = z - p.halo
            ra, rb = ra_ref[i].astype(F32), rb_ref[i].astype(F32)
            left = jnp.where(has_left, jnp.where(even, rb, ra), 0.0)
            right = jnp.where(has_right, jnp.where(even, ra, rb), 0.0)
            plane = jnp.concatenate([left, own_ref[i].astype(F32), right], axis=0)
        for e in range(taps):
            moved = lane_shift(plane, e, reach, lane).astype(BF16)
            for w in range(p.windows):
                xs_ref[w, e * 32 : e * 32 + 32, z * nx : (z + 1) * nx] = moved[16 * w : 16 * w + 32]

    z_low = jnp.where(has_below, 0, reach)
    z_high = jnp.where(has_above, p.ez, p.ez - reach)
    u_row = lax.broadcasted_iota(jnp.int32, (p.ey, nx), 0)
    lane16 = lax.broadcasted_iota(jnp.int32, (16, nx), 1)

    def visit(t, k, rank):
        block, view = pairs_ref[2 * t], pairs_ref[2 * t + 1]
        bl = lax.rem(lax.rem(block, p.row_blocks), p.blocks)
        kid = ids_ref[block * p.views + view]
        if p.fast:
            x = (kid // p.n_gz) ^ b
            at = jnp.where(lax.rem(kid, p.n_gz) == g, 0, p.n_blk) + (x ^ (x >> 1))
            at = at * p.views_here + (view - v * p.views_here)
        else:
            at = (view - v * p.views_here) * p.n_sets + kid
        w, odd = bl // 2, lax.rem(bl, 2)
        for kk in range(p.n_blk):

            @pl.when(k == kk)
            def _():
                tile_ref[...] = arrived[kk][rank]

        base = kf_ref[pl.ds(pl.multiple_of(at * 8, 8), 8), :]
        base = jnp.where(odd == 1, pltpu.roll(base, 10, 1), pltpu.roll(base, 2, 1))
        wf = [
            pltpu.roll(jnp.broadcast_to(base[a : a + 1], (16, 256)), 0, 1, stride=1, stride_axis=0)
            for a in range(taps)
        ]
        wf = jnp.concatenate(wf, axis=0).astype(BF16)
        base = kb_ref[pl.ds(pl.multiple_of(at * 8, 8), 8), :]
        wb = [
            pltpu.roll(jnp.broadcast_to(base[a : a + 1], (8, 128)), 0, 1, stride=1, stride_axis=0)
            for a in range(taps)
        ]
        wb = jnp.concatenate(wb, axis=0).astype(BF16)

        y_first = lax.rem(block, p.row_blocks) * p.by - reach
        y_ok = (u_row + y_first >= 0) & (u_row + y_first < p.row_blocks * p.by)
        acc = {}
        for pair in range(p.zz // 2):
            got = jnp.dot(wf, xs_ref[w, :, pair * 2 * nx : (pair + 1) * 2 * nx], preferred_element_type=F32)
            for half in range(2):
                z = pair * 2 + half
                for a in range(taps):
                    s = z - a
                    if 0 <= s < p.ez:
                        part = got[16 * a : 16 * a + 16, half * nx : (half + 1) * nx]
                        acc[s] = part if s not in acc else acc[s] + part
                s = z - taps + 1
                if 0 <= s < p.ez:
                    z_ok = (s >= z_low) & (s < z_high)
                    ratio = tile_ref[s].astype(F32) / acc[s][: p.ey]
                    r_ref[s, : p.ey, :] = jnp.where(y_ok & z_ok, ratio, 0.0)
                    full = r_ref[s]
                    for e in range(taps):
                        r2_ref[e * 16 : e * 16 + 16, s * nx : (s + 1) * nx] = lane_shift(
                            full, e, reach, lane16
                        ).astype(BF16)
        term = {}
        for pair in range(p.ez // 2):
            got = jnp.dot(wb, r2_ref[:, pair * 2 * nx : (pair + 1) * 2 * nx], preferred_element_type=F32)
            for half in range(2):
                s = pair * 2 + half
                for a in range(taps):
                    z = s + a - 2 * reach
                    if 0 <= z < p.cz:
                        part = got[8 * a : 8 * a + 8, half * nx : (half + 1) * nx]
                        term[z] = part if z not in term else term[z] + part
        for z in range(p.cz):
            at_y = pl.ds(pl.multiple_of(bl * 8, 8), 8)
            out_ref[z, at_y, :] = out_ref[z, at_y, :] + term[z]

    def from_source(k, carry):
        src = lax.rem(b - k + p.n_blk, p.n_blk)
        first = ((src * p.n_gz + g) * p.n_view + v) * p.tiles

        def one(j, rank):
            home = lax.rem(pairs_ref[2 * (first + j)], p.row_blocks) // p.blocks
            mine = home == b

            @pl.when(mine)
            def _():
                visit(first + j, k, rank)

            return rank + mine.astype(jnp.int32)

        lax.fori_loop(0, p.tiles, one, jnp.int32(0))
        return carry

    lax.fori_loop(0, p.n_blk, from_source, 0)


def corrections(p, pairs, ids, pieces, kern, arrived):
    return pl.pallas_call(
        functools.partial(tiles_kernel, p),
        out_shape=jax.ShapeDtypeStruct((p.cz, p.ly, p.nx), F32),
        in_specs=[SM, SM] + [VM] * (6 + p.n_blk),
        out_specs=VM,
        scratch_shapes=[
            pltpu.VMEM((p.windows, 256, p.zz * p.nx), BF16),
            pltpu.VMEM((kern.shape[0], 256), F32),
            pltpu.VMEM((kern.shape[0], 128), F32),
            pltpu.VMEM((p.ez, p.ey, p.nx), BF16),
            pltpu.VMEM((p.ez, 16, p.nx), F32),
            pltpu.VMEM((128, p.ez * p.nx), BF16),
        ],
        name="tiles",
    )(pairs, ids, *pieces, kern, *arrived)


def on_device(estimate, view_tiles, tile_pairs, kernel_table, kernel_ids):
    p = Plan(estimate, view_tiles, tile_pairs, kernel_table, kernel_ids)
    b, g, v = ranks()
    pairs = tile_pairs.reshape(-1)
    ids = kernel_ids.reshape(-1)
    first_block = g * p.row_blocks + b * p.blocks
    own_blocks = first_block + jnp.arange(p.blocks, dtype=jnp.int32)
    count = jnp.sum((tile_pairs[None, :, 0] == own_blocks[:, None]).astype(F32), axis=1)

    kern = kernel_table.reshape(p.views_here * p.sets_here, p.taps, p.taps * p.taps)
    kern = jnp.pad(kern, ((0, 0), (0, 1), (0, 128 - p.taps * p.taps)))
    if not p.fast:
        kern = kern.reshape(p.views_here, p.sets_here * 8, 128)
        kern = lax.all_gather(kern, ("blk", "gz"), axis=1, tiled=True)
    kern = kern.reshape(-1, 128)

    pieces, gathered = halos(p, *first_sends(p, estimate), kern)
    kern = gathered if p.fast else kern
    packed = pack(p, pairs, view_tiles)
    arrived = [packed[0]] + [
        lax.ppermute(packed[k], "blk", [(i, (i + k) % p.n_blk) for i in range(p.n_blk)])
        for k in range(1, p.n_blk)
    ]
    current = estimate
    for iteration in range(ITERS):
        mine = corrections(p, pairs, ids, pieces, kern, arrived)
        other = lax.ppermute(mine, "view", [(0, 1), (1, 0)])
        last = iteration == ITERS - 1
        out = update(p, count, current, mine, other, last)
        current = out[0]
        if not last:
            pieces, _ = halos(p, *out[1:])
    return current


def solution(mesh):
    in_specs = (
        P(("group", "gz"), "blk", None),
        P(("group", "blk", "gz", "view"), None, None, None),
        P("group", None),
        P("view", ("group", "blk", "gz"), None, None, None),
        P("group", None),
    )
    out_specs = P(("group", "gz"), "blk", None)
    return jax.shard_map(
        on_device, mesh=mesh, in_specs=in_specs, out_specs=out_specs, check_vma=False
    )
```

```python
import functools

import jax
import jax.numpy as jnp
from jax import lax
from jax.experimental import pallas as pl
from jax.experimental.pallas import tpu as pltpu
from jax.sharding import PartitionSpec as P


ITERS = 2
F32, BF16 = jnp.float32, jnp.bfloat16
VM = pl.BlockSpec(memory_space=pltpu.VMEM)
SM = pl.BlockSpec(memory_space=pltpu.SMEM)


def send_order(n_blk):
    return sorted(range(1, n_blk), key=lambda k: (k < n_blk // 2, k))


class Plan:
    def __init__(self, estimate, view_tiles, kernel_table):
        self.cz, self.ly, self.nx = estimate.shape
        self.tiles, self.ez, self.ey, _ = view_tiles.shape
        self.views_here, self.sets_here, self.taps = kernel_table.shape[:3]
        self.reach = (self.taps - 1) // 2
        self.by = self.ey - 2 * self.reach
        self.blocks = self.ly // self.by
        self.n_blk = lax.axis_size("blk")
        self.n_gz = lax.axis_size("gz")
        self.n_view = lax.axis_size("view")
        self.views = self.views_here * self.n_view
        self.row_blocks = self.blocks * self.n_blk
        self.slots = -(-self.views_here * self.blocks // self.n_blk)
        self.slots = min(self.slots, self.tiles)
        self.fast = self.n_blk == 4 and self.n_gz == 2 and self.sets_here == 1
        self.n_sets = self.n_blk * self.n_gz * self.sets_here
        self.halo = 2 * self.reach
        assert self.by == 8 and self.cz == 8 and self.nx == 128 and self.taps == 7
        assert self.n_blk & (self.n_blk - 1) == 0 and self.n_blk > 1 and self.ez <= 16
        self.zz = self.cz + 2 * self.halo
        self.rows = self.ly + 16
        self.yw = 24
        self.depth = (self.taps * self.yw + 15) // 16 * 16
        self.send_order = send_order(self.n_blk)


def ranks():
    return lax.axis_index("blk"), lax.axis_index("gz"), lax.axis_index("view")


def lane_shift(plane, e, reach, lane):
    d = e - reach
    if d == 0:
        return plane
    n = plane.shape[-1]
    rolled = pltpu.roll(plane, (-d) % n, 1)
    ok = (lane < n - d) if d > 0 else (lane >= -d)
    return jnp.where(ok, rolled, 0.0)


def pack_kernel(p, pairs_ref, tiles_ref, *outs):
    b, g, v = ranks()
    first = ((b * p.n_gz + g) * p.n_view + v) * p.tiles
    homes = [(pairs_ref[2 * (first + j)] % p.row_blocks) // p.blocks for j in range(p.tiles)]
    for j in range(p.tiles):
        rank = sum([(homes[i] == homes[j]).astype(jnp.int32) for i in range(j)], jnp.int32(0))
        k = homes[j] ^ b
        for kk in range(p.n_blk):

            @pl.when(k == kk)
            def _():
                for s in range(p.ez):
                    outs[kk][rank, s * p.ey : (s + 1) * p.ey, :] = tiles_ref[j, s]


def pack(p, pairs, tiles):
    return pl.pallas_call(
        functools.partial(pack_kernel, p),
        out_shape=[jax.ShapeDtypeStruct((p.slots, p.ez * p.ey, p.nx), tiles.dtype)] * p.n_blk,
        in_specs=[SM, VM],
        out_specs=[VM] * p.n_blk,
        name="pack", compiler_params=pltpu.CompilerParams(vmem_limit_bytes=4 << 20),
    )(pairs, tiles)


def sends_of(p, b, x, own_ref, sa_ref, sb_ref):
    even = b % 2 == 0
    for z in range(p.cz):
        xb = x[z].astype(BF16)
        own_ref[z] = xb
        lo, hi = xb[:8], xb[p.ly - 8 :]
        lo, hi = x[z][:8], x[z][p.ly - 8 :]
        sa_ref[z] = jnp.where(even, hi, lo).astype(BF16)
        sb_ref[z] = jnp.where(even, lo, hi).astype(BF16)


def first_kernel(p, est_ref, own_ref, sa_ref, sb_ref):
    b, _, _ = ranks()
    sends_of(p, b, [est_ref[z] for z in range(p.cz)], own_ref, sa_ref, sb_ref)


def update_kernel(p, count_ref, est_ref, mine_ref, other_ref, new_ref, own_ref=None, sa_ref=None, sb_ref=None):
    b, _, _ = ranks()
    x = []
    for z in range(p.cz):
        rows = []
        for k in range(p.blocks):
            at = slice(k * 8, k * 8 + 8)
            total = mine_ref[z, at, :] + other_ref[z, at, :]
            rows.append(est_ref[z, at, :] * total / count_ref[k])
        x.append(jnp.concatenate(rows, axis=0))
        new_ref[z] = x[z]
    if own_ref is not None:
        sends_of(p, b, x, own_ref, sa_ref, sb_ref)


def sends_shape(p):
    return [
        jax.ShapeDtypeStruct((p.cz, p.ly, p.nx), BF16),
        jax.ShapeDtypeStruct((p.cz, 8, p.nx), BF16),
        jax.ShapeDtypeStruct((p.cz, 8, p.nx), BF16),
    ]


def first_sends(p, est):
    return pl.pallas_call(
        functools.partial(first_kernel, p), out_shape=sends_shape(p), in_specs=[VM],
        out_specs=[VM] * 3, name="first", compiler_params=pltpu.CompilerParams(vmem_limit_bytes=4 << 20),
    )(est)


def update(p, count, est, mine, other, last):
    shapes = [jax.ShapeDtypeStruct(est.shape, F32)] + ([] if last else sends_shape(p))
    return pl.pallas_call(
        functools.partial(update_kernel, p), out_shape=shapes, in_specs=[SM, VM, VM, VM],
        out_specs=[VM] * len(shapes), name="update", compiler_params=pltpu.CompilerParams(vmem_limit_bytes=4 << 20),
    )(count, est, mine, other)


def edges_kernel(p, own_ref, ra_ref, rb_ref, lo_ref, hi_ref=None):
    b, g, _ = ranks()
    even = b % 2 == 0
    has_lo, has_hi = b > 0, b < p.n_blk - 1

    def planes(out_ref, start):
        for i in range(p.halo):
            ra, rb = ra_ref[start + i].astype(F32), rb_ref[start + i].astype(F32)
            left = jnp.where(has_lo, jnp.where(even, rb, ra), 0.0)
            right = jnp.where(has_hi, jnp.where(even, ra, rb), 0.0)
            out_ref[i, :8] = left.astype(BF16)
            out_ref[i, 8 : 8 + p.ly] = own_ref[start + i]
            out_ref[i, 8 + p.ly :] = right.astype(BF16)

    if hi_ref is None:
        planes(lo_ref, jnp.where(g == 0, p.cz - p.halo, 0))
    else:
        planes(lo_ref, p.cz - p.halo)
        planes(hi_ref, 0)


def pairs_of(n):
    pair = [(i, i ^ 1) for i in range(n)]
    odd = [(i, (i + 1) % n if i % 2 else (i - 1) % n) for i in range(n)]
    return pair, odd


def halos(p, own, sa, sb, kern=None):
    pair, odd = pairs_of(p.n_blk)
    nz = p.cz * 8
    carry = kern is not None and p.fast
    if carry:
        got = lax.ppermute(jnp.concatenate([sa.reshape(nz, p.nx), kern]), "blk", pair)
        ra, kern = got[:nz].reshape(sa.shape), jnp.concatenate([kern, got[nz:]])
        got = lax.ppermute(jnp.concatenate([sb.reshape(nz, p.nx), kern]), "blk", odd)
        rb, kern = got[:nz].reshape(sb.shape), jnp.concatenate([kern, got[nz:]])
    else:
        ra, rb = lax.ppermute(sa, "blk", pair), lax.ppermute(sb, "blk", odd)
    two = p.n_gz == 2
    edge = jax.ShapeDtypeStruct((p.halo, p.rows, p.nx), BF16)
    out = pl.pallas_call(
        functools.partial(edges_kernel, p), out_shape=[edge] if two else [edge, edge],
        in_specs=[VM] * 3, out_specs=[VM] * (1 if two else 2), name="edges",
        compiler_params=pltpu.CompilerParams(vmem_limit_bytes=4 << 20),
    )(own, ra, rb)
    if two:
        swap = [(0, 1), (1, 0)]
        if carry:
            ne = p.halo * p.rows
            got = lax.ppermute(jnp.concatenate([out[0].reshape(ne, p.nx), kern]), "gz", swap)
            below = above = got[:ne].reshape(edge.shape)
            kern = jnp.concatenate([kern, got[ne:]])
        else:
            below = above = lax.ppermute(out[0], "gz", swap)
    else:
        ups = [(i, i + 1) for i in range(p.n_gz - 1)]
        below = lax.ppermute(out[0], "gz", ups)
        above = lax.ppermute(out[1], "gz", [(j, i) for i, j in ups])
    return (own, ra, rb, below, above), kern


def blur_kernel(p, ids_ref, own_ref, ra_ref, rb_ref, below_ref, above_ref, kern_ref, *rest):
    first = len(rest) == 4
    out_ref, kb_ref, xs_ref, kf_ref = rest if first else (rest[0], None, *rest[1:])
    taps, nx, yw = p.taps, p.nx, p.yw
    row = lax.broadcasted_iota(jnp.int32, (128, 256), 0)
    col = lax.broadcasted_iota(jnp.int32, (128, 256), 1)
    select = ((row // taps == col % yw) & (row % taps == col // yw) & (row < taps * taps)).astype(BF16)
    kf_ref[...] = jnp.dot(kern_ref[...], select, preferred_element_type=F32)
    if first:
        row = lax.broadcasted_iota(jnp.int32, (128, 128), 0)
        col = lax.broadcasted_iota(jnp.int32, (128, 128), 1)
        select = (
            (taps - 1 - row // taps == col % 16) & (taps - 1 - row % taps == col // 16) & (row < taps * taps)
        ).astype(BF16)
        kb_ref[...] = jnp.dot(kern_ref[...], select, preferred_element_type=F32)

    b, g, _ = ranks()
    even = b % 2 == 0
    has_left, has_right = b > 0, b < p.n_blk - 1
    has_below, has_above = g > 0, g < p.n_gz - 1
    lane = lax.broadcasted_iota(jnp.int32, (p.rows, nx), 1)
    for z in range(p.zz):
        i = z - p.halo
        if i < 0:
            plane = jnp.where(has_below, below_ref[z].astype(F32), 0.0)
        elif i >= p.cz:
            plane = jnp.where(has_above, above_ref[i - p.cz].astype(F32), 0.0)
        else:
            ra, rb = ra_ref[i].astype(F32), rb_ref[i].astype(F32)
            left = jnp.where(has_left, jnp.where(even, rb, ra), 0.0)
            right = jnp.where(has_right, jnp.where(even, ra, rb), 0.0)
            plane = jnp.concatenate([left, own_ref[i].astype(F32), right], axis=0)
        moved = [lane_shift(plane, e, p.reach, lane) for e in range(taps)] + [jnp.zeros_like(plane)]
        for bl in range(p.blocks):
            for e in range(0, taps, 2):
                at = slice(8 * bl, 8 * bl + yw)
                high = moved[e + 1][at] if e + 1 < taps else jnp.zeros((p.depth - e * yw - yw, nx), F32)
                both = jnp.concatenate([moved[e][at], high], axis=0).astype(BF16)
                xs_ref[bl, e * yw : e * yw + both.shape[0], z * nx : (z + 1) * nx] = both

    def block(bl, carry):
        wf = [[] for _ in range(taps)]
        for view in range(p.views_here):
            base = pltpu.roll(kf_ref[kernel_rows(p, ids_ref, bl, view), :], 2, 1)
            for a in range(taps):
                wide = jnp.broadcast_to(base[a : a + 1], (16, 256))
                wf[a].append(pltpu.roll(wide, 0, 1, stride=1, stride_axis=0))
        wf = jnp.concatenate([x for y in wf for x in y], axis=0).astype(BF16)[:, : p.depth]
        m = 16 * p.views_here
        acc = {}
        for pair in range(p.zz // 2):
            z0 = pair * 2
            lo, hi = max(0, z0 - p.ez + 1), min(taps - 1, z0 + 1)
            got = jnp.dot(
                wf[m * lo : m * (hi + 1)], xs_ref[bl, :, z0 * nx : (z0 + 2) * nx], preferred_element_type=F32
            )
            for half in range(2):
                z = z0 + half
                for a in range(lo, hi + 1):
                    s = z - a
                    if 0 <= s < p.ez:
                        part = got[m * (a - lo) : m * (a - lo + 1), half * nx : (half + 1) * nx]
                        acc[s] = part if s not in acc else acc[s] + part
                s = z - taps + 1
                if 0 <= s < p.ez:
                    done = acc.pop(s)
                    for view in range(p.views_here):
                        out_ref[bl * p.views_here + view, s] = done[16 * view : 16 * view + 16]
        return carry

    lax.fori_loop(0, p.blocks, block, 0)


def kernel_rows(p, ids_ref, bl, view):
    b, g, v = ranks()
    number = g * p.row_blocks + b * p.blocks + bl
    kid = ids_ref[number * p.views + v * p.views_here + view]
    if p.fast:
        x = (kid // p.n_gz) ^ b
        at = jnp.where(lax.rem(kid, p.n_gz) == g, 0, p.n_blk) + (x ^ (x >> 1))
        at = at * p.views_here + view
    else:
        at = view * p.n_sets + kid
    return pl.ds(pl.multiple_of(at * 8, 8), 8)


def blur(p, ids, pieces, kern, first):
    blurred = jax.ShapeDtypeStruct((p.blocks * p.views_here, p.ez, 16, p.nx), F32)
    table = jax.ShapeDtypeStruct((kern.shape[0], 128), F32)
    ins = [ids, *pieces, kern]
    return pl.pallas_call(
        functools.partial(blur_kernel, p),
        out_shape=[blurred, table] if first else [blurred],
        in_specs=[SM] + [VM] * (len(ins) - 1),
        out_specs=[VM] * (2 if first else 1),
        scratch_shapes=[
            pltpu.VMEM((p.blocks, p.depth, p.zz * p.nx), BF16),
            pltpu.VMEM((kern.shape[0], 256), F32),
        ],
        name="blur", compiler_params=pltpu.CompilerParams(vmem_limit_bytes=10 << 20),
    )(*ins)


def spread_kernel(p, pairs_ref, ids_ref, blur_ref, kb_ref, tiles_ref, out_ref, slot_ref, r_ref, r2_ref):
    b, g, v = ranks()
    taps, reach, nx, views = p.taps, p.reach, p.nx, p.views_here
    r_ref[...] = jnp.zeros(r_ref.shape, F32)
    for view in range(views):
        r2_ref[view * 128 + taps * 16 : (view + 1) * 128, :] = jnp.zeros((128 - taps * 16, r2_ref.shape[1]), BF16)
    has_below, has_above = g > 0, g < p.n_gz - 1
    z_low = jnp.where(has_below, 0, reach)
    z_high = jnp.where(has_above, p.ez, p.ez - reach)
    u_row = lax.broadcasted_iota(jnp.int32, (p.ey, nx), 0)
    lane16 = lax.broadcasted_iota(jnp.int32, (16, nx), 1)

    for i in range(p.blocks * views):
        slot_ref[i] = -1

    def from_source(k, carry):
        first = (((b ^ k) * p.n_gz + g) * p.n_view + v) * p.tiles
        rank = jnp.int32(0)
        for j in range(p.tiles):
            place = lax.rem(pairs_ref[2 * (first + j)], p.row_blocks)
            mine = place // p.blocks == b
            at = lax.rem(place, p.blocks) * views + pairs_ref[2 * (first + j) + 1] - v * views
            at = jnp.where(mine, at, p.blocks * views)
            slot_ref[at] = k * p.slots + rank
            rank = rank + mine.astype(jnp.int32)
        return carry

    lax.fori_loop(0, p.n_blk, from_source, 0)

    def block(bl, carry):
        wb = []
        for view in range(views):
            base = kb_ref[kernel_rows(p, ids_ref, bl, view), :]
            rows = [
                pltpu.roll(jnp.broadcast_to(base[a : a + 1], (8, 128)), 0, 1, stride=1, stride_axis=0)
                for a in range(taps)
            ]
            wb.append(jnp.concatenate(rows + [jnp.zeros((8, 128), F32)], axis=0))
        wb = jnp.concatenate(wb, axis=1).astype(BF16)
        y_first = (b * p.blocks + bl) * p.by - reach
        y_ok = (u_row + y_first >= 0) & (u_row + y_first < p.row_blocks * p.by)
        slots = [slot_ref[bl * views + view] for view in range(views)]
        term = {}
        for pair in range(p.ez // 2):
            s0 = pair * 2
            for s in (s0, s0 + 1):
                z_ok = (s >= z_low) & (s < z_high)
                for view in range(views):
                    tile = tiles_ref[jnp.maximum(slots[view], 0), s * p.ey : (s + 1) * p.ey, :].astype(F32)
                    ratio = tile / blur_ref[bl * views + view, s, : p.ey, :]
                    keep = y_ok & (z_ok & (slots[view] >= 0))
                    r_ref[view, s, : p.ey, :] = jnp.where(keep, ratio, 0.0)
                    full = r_ref[view, s]
                    for e in range(taps):
                        at = view * 128 + e * 16
                        r2_ref[at : at + 16, s * nx : (s + 1) * nx] = lane_shift(full, e, reach, lane16).astype(BF16)
            lo, hi = max(0, 2 * reach - s0 - 1) // 2 * 2, min(taps - 1, 2 * reach + p.cz - 1 - s0) // 2 * 2 + 1
            got = jnp.dot(
                wb[8 * lo : 8 * hi + 8], r2_ref[:, s0 * nx : (s0 + 2) * nx], preferred_element_type=F32
            )
            for half in range(2):
                s = s0 + half
                for a in range(lo, min(hi, taps - 1) + 1):
                    z = s + a - 2 * reach
                    if 0 <= z < p.cz:
                        at_a = 8 * (a - lo)
                        part = got[at_a : at_a + 8, half * nx : (half + 1) * nx]
                        term[z] = part if z not in term else term[z] + part
        for z in range(p.cz):
            out_ref[z, pl.ds(pl.multiple_of(bl * 8, 8), 8), :] = term[z]
        return carry

    lax.fori_loop(0, p.blocks, block, 0)


def spread(p, pairs, ids, blurred, table, arrived):
    ins = [pairs, ids, blurred, table, arrived]
    return pl.pallas_call(
        functools.partial(spread_kernel, p),
        out_shape=jax.ShapeDtypeStruct((p.cz, p.ly, p.nx), F32),
        in_specs=[SM, SM] + [VM] * (len(ins) - 2),
        out_specs=VM,
        scratch_shapes=[
            pltpu.SMEM((p.blocks * p.views_here + 1,), jnp.int32),
            pltpu.VMEM((p.views_here, p.ez, 16, p.nx), F32),
            pltpu.VMEM((p.views_here * 128, p.ez * p.nx), BF16),
        ],
        name="spread", compiler_params=pltpu.CompilerParams(vmem_limit_bytes=6 << 20),
    )(*ins)


def on_device(estimate, view_tiles, tile_pairs, kernel_table, kernel_ids):
    p = Plan(estimate, view_tiles, kernel_table)
    b, g, _ = ranks()
    pairs = tile_pairs.reshape(-1)
    ids = kernel_ids.reshape(-1)
    first_block = g * p.row_blocks + b * p.blocks
    own_blocks = first_block + jnp.arange(p.blocks, dtype=jnp.int32)
    count = jnp.sum((tile_pairs[None, :, 0] == own_blocks[:, None]).astype(F32), axis=1)

    kern = kernel_table.reshape(p.views_here * p.sets_here, p.taps, p.taps * p.taps)
    kern = jnp.pad(kern, ((0, 0), (0, 1), (0, 128 - p.taps * p.taps)))
    if not p.fast:
        kern = kern.reshape(p.views_here, p.sets_here * 8, 128)
        kern = lax.all_gather(kern, ("blk", "gz"), axis=1, tiled=True)
    kern = kern.reshape(-1, 128)

    pieces, gathered = halos(p, *first_sends(p, estimate), kern)
    kern = gathered if p.fast else kern
    packed = pack(p, pairs, view_tiles)
    arrived = [packed[0]] + [None] * (p.n_blk - 1)
    for k in p.send_order:
        arrived[k] = lax.ppermute(packed[k], "blk", [(i, i ^ k) for i in range(p.n_blk)])
    blurred, table = blur(p, ids, pieces, kern, True)
    arrived = jnp.concatenate(arrived)
    current = estimate
    for iteration in range(ITERS):
        last = iteration == ITERS - 1
        mine = spread(p, pairs, ids, blurred, table, arrived)
        other = lax.ppermute(mine, "view", [(0, 1), (1, 0)])
        out = update(p, count, current, mine, other, last)
        current = out[0]
        if not last:
            pieces, _ = halos(p, *out[1:])
            blurred = blur(p, ids, pieces, kern, False)[0]
    return current


def solution(mesh):
    in_specs = (
        P(("group", "gz"), "blk", None),
        P(("group", "blk", "gz", "view"), None, None, None),
        P("group", None),
        P("view", ("group", "blk", "gz"), None, None, None),
        P("group", None),
    )
    out_specs = P(("group", "gz"), "blk", None)
    return jax.shard_map(
        on_device, mesh=mesh, in_specs=in_specs, out_specs=out_specs, check_vma=False
    )
```

```python
import functools

import jax
import jax.numpy as jnp
from jax import lax
from jax.experimental import pallas as pl
from jax.experimental.pallas import tpu as pltpu
from jax.sharding import PartitionSpec as P


ITERS = 2
F32, BF16 = jnp.float32, jnp.bfloat16
VM = pl.BlockSpec(memory_space=pltpu.VMEM)
SM = pl.BlockSpec(memory_space=pltpu.SMEM)


def send_order(n_blk):
    return sorted(range(1, n_blk), key=lambda k: (k < n_blk // 2, k))


class Plan:
    def __init__(self, estimate, view_tiles, kernel_table):
        self.cz, self.ly, self.nx = estimate.shape
        self.tiles, self.ez, self.ey, _ = view_tiles.shape
        self.views_here, self.sets_here, self.taps = kernel_table.shape[:3]
        self.reach = (self.taps - 1) // 2
        self.by = self.ey - 2 * self.reach
        self.blocks = self.ly // self.by
        self.n_blk = lax.axis_size("blk")
        self.n_gz = lax.axis_size("gz")
        self.n_view = lax.axis_size("view")
        self.row_blocks = self.blocks * self.n_blk
        self.slots = -(-self.views_here * self.blocks // self.n_blk)
        self.slots = min(self.slots, self.tiles)
        self.fast = self.n_blk == 4 and self.n_gz == 2 and self.sets_here == 1
        self.n_sets = self.n_blk * self.n_gz * self.sets_here
        self.halo = 2 * self.reach
        assert self.by == 8 and self.cz == 8 and self.nx == 128 and self.taps == 7
        assert self.n_blk & (self.n_blk - 1) == 0 and self.n_blk > 1 and self.ez <= 16
        self.zz = self.cz + 2 * self.halo
        self.rows = self.ly + 16
        self.yw = 24
        self.depth = (self.taps * self.yw + 15) // 16 * 16
        self.send_order = send_order(self.n_blk)


def ranks():
    return lax.axis_index("blk"), lax.axis_index("gz"), lax.axis_index("view")


def lane_shift(plane, e, reach, lane):
    d = e - reach
    if d == 0:
        return plane
    n = plane.shape[-1]
    rolled = pltpu.roll(plane, (-d) % n, 1)
    ok = (lane < n - d) if d > 0 else (lane >= -d)
    return jnp.where(ok, rolled, jnp.zeros_like(rolled))


def sends_of(p, b, x, own_ref, sa_ref, sb_ref):
    even = b % 2 == 0
    for z in range(p.cz):
        xb = x[z].astype(BF16)
        own_ref[z] = xb
        lo, hi = xb[:8], xb[p.ly - 8 :]
        lo, hi = x[z][:8], x[z][p.ly - 8 :]
        sa_ref[z] = jnp.where(even, hi, lo).astype(BF16)
        sb_ref[z] = jnp.where(even, lo, hi).astype(BF16)


def first_kernel(p, pairs_hbm, est_hbm, tiles_hbm, table_hbm, *refs):
    own_ref, sa_ref, sb_ref, kern_ref, count_ref, *packed = refs[: 5 + p.n_blk]
    pairs_ref, blocks_ref, est_ref, tiles_ref, table_ref, sems = refs[5 + p.n_blk :]
    moves = [(est_hbm, est_ref), (table_hbm, table_ref), (pairs_hbm, pairs_ref), (pairs_hbm, blocks_ref), (tiles_hbm, tiles_ref)]
    copies = [pltpu.make_async_copy(i, j, sems.at[n]) for n, (i, j) in enumerate(moves)]
    for copy in copies:
        copy.start()
    b, g, v = ranks()
    copies[0].wait()
    sends_of(p, b, [est_ref[z] for z in range(p.cz)], own_ref, sa_ref, sb_ref)
    copies[1].wait()
    kern_ref[...] = jnp.zeros(kern_ref.shape, BF16)
    if p.sets_here == 1:
        for i in range(p.views_here):
            cube = table_ref[i, 0].astype(F32)
            rows = jnp.concatenate([cube[:, c, :] for c in range(p.taps)], axis=1)
            rows = jnp.concatenate([rows, jnp.zeros((p.taps, 128 - p.taps * p.taps), F32)], axis=1)
            rows = jnp.concatenate([rows, jnp.zeros((8 - p.taps, 128), F32)], axis=0)
            kern_ref[8 * i : 8 * i + 8, :] = rows.astype(BF16)

    copies[2].wait()
    copies[3].wait()
    for k in range(p.blocks):
        same = blocks_ref[0:1, :] == g * p.row_blocks + b * p.blocks + k
        count = jnp.sum(jnp.where(same, 1.0, 0.0), axis=1, keepdims=True)
        count_ref[8 * k : 8 * k + 8, :] = jnp.broadcast_to(count, (8, p.nx))
    copies[4].wait()
    first = ((b * p.n_gz + g) * p.n_view + v) * p.tiles
    homes = [lax.rem(pairs_ref[0, first + j], p.row_blocks) // p.blocks for j in range(p.tiles)]
    for j in range(p.tiles):
        rank = sum([(homes[i] == homes[j]).astype(jnp.int32) for i in range(j)], jnp.int32(0))
        for k in range(p.n_blk):

            @pl.when(homes[j] ^ b == k)
            def _():
                for s in range(p.ez):
                    packed[k][rank, s * p.ey : (s + 1) * p.ey, :] = tiles_ref[j, s]


def slots_kernel(p, pairs_ref, after_ref, slot_ref):
    b, g, v = ranks()
    for i in range(p.blocks * p.views_here):
        slot_ref[i] = -1

    def from_source(k, carry):
        first = (((b ^ k) * p.n_gz + g) * p.n_view + v) * p.tiles
        rank = jnp.int32(0)
        for j in range(p.tiles):
            place = lax.rem(pairs_ref[0, first + j], p.row_blocks)
            mine = place // p.blocks == b
            at = lax.rem(place, p.blocks) * p.views_here + pairs_ref[1, first + j] - v * p.views_here
            slot_ref[jnp.where(mine, at, p.blocks * p.views_here)] = k * p.slots + rank
            rank = rank + mine.astype(jnp.int32)
        return carry

    lax.fori_loop(0, p.n_blk, from_source, 0)


def slots_of(p, pairs, after):
    return pl.pallas_call(
        functools.partial(slots_kernel, p),
        out_shape=jax.ShapeDtypeStruct((p.blocks * p.views_here + 1,), jnp.int32),
        in_specs=[SM, pl.BlockSpec(memory_space=pl.ANY)], out_specs=SM, name="slots",
        compiler_params=pltpu.CompilerParams(vmem_limit_bytes=1 << 20),
    )(pairs, after)


def update_kernel(p, count_ref, est_ref, mine_ref, other_ref, new_ref, own_ref=None, sa_ref=None, sb_ref=None):
    b, _, _ = ranks()
    x = []
    for z in range(p.cz):
        rows = []
        for k in range(p.blocks):
            at = slice(k * 8, k * 8 + 8)
            total = mine_ref[z, at, :] + other_ref[z, at, :]
            rows.append(est_ref[z, at, :] * total / count_ref[at, :])
        x.append(jnp.concatenate(rows, axis=0))
        new_ref[z] = x[z]
    if own_ref is not None:
        sends_of(p, b, x, own_ref, sa_ref, sb_ref)


def sends_shape(p):
    return [
        jax.ShapeDtypeStruct((p.cz, p.ly, p.nx), BF16),
        jax.ShapeDtypeStruct((p.cz, 8, p.nx), BF16),
        jax.ShapeDtypeStruct((p.cz, 8, p.nx), BF16),
    ]


def first_sends(p, pairs, est, tiles, table):
    shapes = sends_shape(p) + [
        jax.ShapeDtypeStruct((8 * p.views_here, 128), BF16),
        jax.ShapeDtypeStruct((8 * p.blocks, p.nx), F32),
    ]
    shapes += [jax.ShapeDtypeStruct((p.slots, p.ez * p.ey, p.nx), tiles.dtype)] * p.n_blk
    return pl.pallas_call(
        functools.partial(first_kernel, p), out_shape=shapes,
        in_specs=[pl.BlockSpec(memory_space=pltpu.HBM)] * 4,
        out_specs=[VM] * len(shapes), name="first",
        scratch_shapes=[
            pltpu.SMEM(pairs.shape, pairs.dtype), pltpu.VMEM(pairs.shape, pairs.dtype), pltpu.VMEM(est.shape, est.dtype),
            pltpu.VMEM(tiles.shape, tiles.dtype), pltpu.VMEM(table.shape, table.dtype), pltpu.SemaphoreType.DMA((5,)),
        ],
        compiler_params=pltpu.CompilerParams(vmem_limit_bytes=4 << 20),
    )(*[pltpu.with_memory_space_constraint(x, pltpu.HBM) for x in (pairs, est, tiles, table)])


def update(p, count, est, mine, other, last):
    shapes = [jax.ShapeDtypeStruct(est.shape, F32)] + ([] if last else sends_shape(p))
    return pl.pallas_call(
        functools.partial(update_kernel, p), out_shape=shapes, in_specs=[VM] * 4,
        out_specs=[VM] * len(shapes), name="update", compiler_params=pltpu.CompilerParams(vmem_limit_bytes=4 << 20),
    )(count, est, mine, other)


def edges_kernel(p, own_ref, ra_ref, rb_ref, lo_ref, hi_ref=None):
    b, g, _ = ranks()
    even = b % 2 == 0
    has_lo, has_hi = b > 0, b < p.n_blk - 1

    def planes(out_ref, start):
        for i in range(p.halo):
            ra, rb = ra_ref[start + i].astype(F32), rb_ref[start + i].astype(F32)
            left = jnp.where(has_lo, jnp.where(even, rb, ra), 0.0)
            right = jnp.where(has_hi, jnp.where(even, ra, rb), 0.0)
            out_ref[i, :8] = left.astype(BF16)
            out_ref[i, 8 : 8 + p.ly] = own_ref[start + i]
            out_ref[i, 8 + p.ly :] = right.astype(BF16)

    if hi_ref is None:
        planes(lo_ref, jnp.where(g == 0, p.cz - p.halo, 0))
    else:
        planes(lo_ref, p.cz - p.halo)
        planes(hi_ref, 0)


def pairs_of(n):
    pair = [(i, i ^ 1) for i in range(n)]
    odd = [(i, (i + 1) % n if i % 2 else (i - 1) % n) for i in range(n)]
    return pair, odd


def halos(p, own, sa, sb, kern=None):
    pair, odd = pairs_of(p.n_blk)
    nz = p.cz * 8
    carry = kern is not None and p.fast
    if carry:
        a = lax.ppermute(jnp.concatenate([sa.reshape(nz, p.nx), kern]), "blk", pair)
        b = lax.ppermute(jnp.concatenate([sb.reshape(nz, p.nx), kern]), "blk", odd)
        c = lax.ppermute(kern, "blk", [(i, i ^ 2) for i in range(p.n_blk)])
        ra, rb = a[:nz].reshape(sa.shape), b[:nz].reshape(sb.shape)
        kern = jnp.concatenate([kern, a[nz:], b[nz:], c])
    else:
        ra, rb = lax.ppermute(sa, "blk", pair), lax.ppermute(sb, "blk", odd)
    two = p.n_gz == 2
    edge = jax.ShapeDtypeStruct((p.halo, p.rows, p.nx), BF16)
    out = pl.pallas_call(
        functools.partial(edges_kernel, p), out_shape=[edge] if two else [edge, edge],
        in_specs=[VM] * 3, out_specs=[VM] * (1 if two else 2), name="edges",
        compiler_params=pltpu.CompilerParams(vmem_limit_bytes=4 << 20),
    )(own, ra, rb)
    if two:
        swap = [(0, 1), (1, 0)]
        if carry:
            ne = p.halo * p.rows
            got = lax.ppermute(jnp.concatenate([out[0].reshape(ne, p.nx), kern]), "gz", swap)
            below = above = got[:ne].reshape(edge.shape)
            kern = jnp.concatenate([kern, got[ne:]])
        else:
            below = above = lax.ppermute(out[0], "gz", swap)
    else:
        ups = [(i, i + 1) for i in range(p.n_gz - 1)]
        below = lax.ppermute(out[0], "gz", ups)
        above = lax.ppermute(out[1], "gz", [(j, i) for i, j in ups])
    return (own, ra, rb, below, above), kern


def blur_kernel(p, ids_ref, own_ref, ra_ref, rb_ref, below_ref, above_ref, kern_ref, *rest):
    first = len(rest) == 4
    out_ref, kb_ref, xs_ref, kf_ref = rest if first else (rest[0], None, *rest[1:])
    taps, nx, yw = p.taps, p.nx, p.yw
    row = lax.broadcasted_iota(jnp.int32, (128, 256), 0)
    col = lax.broadcasted_iota(jnp.int32, (128, 256), 1)
    select = ((row // taps == col % yw) & (row % taps == col // yw) & (row < taps * taps)).astype(BF16)
    kf_ref[...] = jnp.dot(kern_ref[...], select, preferred_element_type=F32)
    if first:
        row = lax.broadcasted_iota(jnp.int32, (128, 128), 0)
        col = lax.broadcasted_iota(jnp.int32, (128, 128), 1)
        for e in range(taps):
            select = (row // taps == taps - 1 - col % 16) & (row % taps == taps - 1 - e)
            select = (select & (row < taps * taps)).astype(BF16)
            kb_ref[e] = jnp.dot(kern_ref[...], select, preferred_element_type=F32)

    b, g, _ = ranks()
    even = b % 2 == 0
    has_left, has_right = b > 0, b < p.n_blk - 1
    has_below, has_above = g > 0, g < p.n_gz - 1
    lane = lax.broadcasted_iota(jnp.int32, (p.rows, nx), 1)
    for z in range(p.zz):
        i = z - p.halo
        if i < 0:
            plane = jnp.where(has_below, below_ref[z].astype(F32), 0.0)
        elif i >= p.cz:
            plane = jnp.where(has_above, above_ref[i - p.cz].astype(F32), 0.0)
        else:
            ra, rb = ra_ref[i].astype(F32), rb_ref[i].astype(F32)
            left = jnp.where(has_left, jnp.where(even, rb, ra), 0.0)
            right = jnp.where(has_right, jnp.where(even, ra, rb), 0.0)
            plane = jnp.concatenate([left, own_ref[i].astype(F32), right], axis=0)
        moved = [lane_shift(plane, e, p.reach, lane) for e in range(taps)] + [jnp.zeros_like(plane)]
        for bl in range(p.blocks):
            for e in range(0, taps, 2):
                at = slice(8 * bl, 8 * bl + yw)
                high = moved[e + 1][at] if e + 1 < taps else jnp.zeros((p.depth - e * yw - yw, nx), F32)
                both = jnp.concatenate([moved[e][at], high], axis=0).astype(BF16)
                xs_ref[bl, z, e * yw : e * yw + both.shape[0], :] = both

    def block(bl, carry):
        wf = [[] for _ in range(taps)]
        for view in range(p.views_here):
            base = pltpu.roll(kf_ref[kernel_rows(p, ids_ref, bl, view), :], 2, 1)
            for a in range(taps):
                wide = jnp.broadcast_to(base[a : a + 1], (16, 256))
                wf[a].append(pltpu.roll(wide, 0, 1, stride=1, stride_axis=0))
        wf = jnp.concatenate([x for y in wf for x in y], axis=0).astype(BF16)[:, : p.depth]
        m = 16 * p.views_here
        acc = {}
        for pair in range(p.zz // 2):
            z0 = pair * 2
            lo, hi = max(0, z0 - p.ez + 1), min(taps - 1, z0 + 1)
            planes = jnp.concatenate([xs_ref[bl, z0], xs_ref[bl, z0 + 1]], axis=1)
            got = jnp.dot(wf[m * lo : m * (hi + 1)], planes, preferred_element_type=F32)
            for half in range(2):
                z = z0 + half
                for a in range(lo, hi + 1):
                    s = z - a
                    if 0 <= s < p.ez:
                        part = got[m * (a - lo) : m * (a - lo + 1), half * nx : (half + 1) * nx]
                        acc[s] = part if s not in acc else acc[s] + part
                s = z - taps + 1
                if 0 <= s < p.ez:
                    done = acc.pop(s)
                    for view in range(p.views_here):
                        out_ref[bl * p.views_here + view, s] = done[16 * view : 16 * view + 16]
        return carry

    for bl in range(p.blocks):
        block(bl, 0)


def kernel_rows(p, ids_ref, bl, view):
    b, g, v = ranks()
    number = g * p.row_blocks + b * p.blocks + bl
    kid = ids_ref[v * p.views_here + view, number]
    if p.fast:
        x = (kid // p.n_gz) ^ b
        at = jnp.where(lax.rem(kid, p.n_gz) == g, 0, p.n_blk) + (x ^ (x >> 1))
        at = at * p.views_here + view
    else:
        at = view * p.n_sets + kid
    return pl.ds(pl.multiple_of(at * 8, 8), 8)


def blur(p, ids, pieces, kern, first):
    blurred = jax.ShapeDtypeStruct((p.blocks * p.views_here, p.ez, 16, p.nx), F32)
    table = jax.ShapeDtypeStruct((p.taps, kern.shape[0], 128), F32)
    ins = [ids, *pieces, kern]
    return pl.pallas_call(
        functools.partial(blur_kernel, p),
        out_shape=[blurred, table] if first else [blurred],
        in_specs=[SM] + [VM] * (len(ins) - 1),
        out_specs=[VM] * (2 if first else 1),
        scratch_shapes=[
            pltpu.VMEM((p.blocks, p.zz, p.depth, p.nx), BF16),
            pltpu.VMEM((kern.shape[0], 256), F32),
        ],
        name="blur", compiler_params=pltpu.CompilerParams(vmem_limit_bytes=10 << 20),
    )(*ins)


def spread_kernel(p, slot_ref, ids_ref, blur_ref, kb_ref, tiles_ref, out_ref, r_ref):
    b, g, _ = ranks()
    taps, reach, nx, views = p.taps, p.reach, p.nx, p.views_here
    has_below, has_above = g > 0, g < p.n_gz - 1
    z_low = jnp.where(has_below, 0, reach)
    z_high = jnp.where(has_above, p.ez, p.ez - reach)
    u_row = lax.broadcasted_iota(jnp.int32, (16, nx), 0)
    lane8 = lax.broadcasted_iota(jnp.int32, (8, nx), 1)

    def block(bl, carry):
        wb = [[] for _ in range(taps)]
        at = [kernel_rows(p, ids_ref, bl, view) for view in range(views)]
        for e in range(taps):
            base = kb_ref[e, at[-1], :]
            for view in range(views - 2, -1, -1):
                base = jnp.where(lane8 < 16 * view + 16, kb_ref[e, at[view], :], base)
            for a in range(taps):
                wide = jnp.broadcast_to(base[a : a + 1], (8, 128))
                wb[a].append(pltpu.roll(wide, 0, 1, stride=1, stride_axis=0))
        wb = jnp.concatenate([x for y in wb for x in y], axis=0).astype(BF16)[:, : 16 * views]
        m = 8 * taps
        y_first = (b * p.blocks + bl) * p.by - reach
        y_ok = (u_row < p.ey) & (u_row + y_first >= 0) & (u_row + y_first < p.row_blocks * p.by)
        slots = [slot_ref[bl * views + view] for view in range(views)]
        acc = {}
        for pair in range(p.ez // 2):
            s0 = pair * 2
            for s in (s0, s0 + 1):
                z_ok = (s >= z_low) & (s < z_high)
                for view in range(views):
                    tile = tiles_ref[jnp.maximum(slots[view], 0), s * p.ey : (s + 1) * p.ey, :].astype(F32)
                    tile = jnp.concatenate([tile, jnp.zeros((16 - p.ey, nx), F32)], axis=0)
                    ratio = tile / blur_ref[bl * views + view, s]
                    keep = y_ok & (z_ok & (slots[view] >= 0))
                    r_ref[bl, s, 16 * view : 16 * view + 16, :] = jnp.where(keep, ratio, 0.0).astype(BF16)
            lo, hi = max(0, 2 * reach - s0 - 1) // 2 * 2, min(taps - 1, 2 * reach + p.cz - 1 - s0)
            planes = jnp.concatenate([r_ref[bl, s0], r_ref[bl, s0 + 1]], axis=1)
            got = jnp.dot(wb[m * lo : m * (hi + 1)], planes, preferred_element_type=F32)
            for half in range(2):
                s = s0 + half
                for a in range(lo, hi + 1):
                    z = s + a - 2 * reach
                    if 0 <= z < p.cz:
                        part = got[m * (a - lo) : m * (a - lo + 1), half * nx : (half + 1) * nx]
                        acc[z] = part if z not in acc else acc[z] + part
                z = s - 2 * reach
                if 0 <= z < p.cz:
                    done = acc.pop(z)
                    term = done[8 * reach : 8 * reach + 8]
                    for e in range(taps):
                        if e != reach:
                            term = term + lane_shift(done[8 * e : 8 * e + 8], e, reach, lane8)
                    out_ref[z, bl * 8 : bl * 8 + 8, :] = term
        return carry

    for bl in range(p.blocks):
        block(bl, 0)


def spread(p, slots, ids, blurred, table, arrived):
    ins = [slots, ids, blurred, table, arrived]
    return pl.pallas_call(
        functools.partial(spread_kernel, p),
        out_shape=jax.ShapeDtypeStruct((p.cz, p.ly, p.nx), F32),
        in_specs=[SM, SM] + [VM] * (len(ins) - 2),
        out_specs=VM,
        scratch_shapes=[
            pltpu.VMEM((p.blocks, p.ez, p.views_here * 16, p.nx), BF16),
        ],
        name="spread", compiler_params=pltpu.CompilerParams(vmem_limit_bytes=6 << 20),
    )(*ins)


def on_device(estimate, view_tiles, tile_pairs, kernel_table, kernel_ids):
    p = Plan(estimate, view_tiles, kernel_table)
    pairs, ids = tile_pairs.T, kernel_ids.T
    own, sa, sb, kern, count, *packed = first_sends(p, pairs, estimate, view_tiles, kernel_table)
    pieces, gathered = halos(p, own, sa, sb, kern)
    if p.fast:
        kern = gathered
    else:
        kern = kernel_table.reshape(p.views_here, p.sets_here, p.taps, p.taps * p.taps)
        kern = jnp.pad(kern, ((0, 0), (0, 0), (0, 1), (0, 128 - p.taps * p.taps)))
        kern = kern.reshape(p.views_here, p.sets_here * 8, 128)
        kern = lax.all_gather(kern, ("blk", "gz"), axis=1, tiled=True).reshape(-1, 128)
    arrived = [packed[0]] + [None] * (p.n_blk - 1)
    for k in p.send_order:
        arrived[k] = lax.ppermute(packed[k], "blk", [(i, i ^ k) for i in range(p.n_blk)])
    blurred, table = blur(p, ids, pieces, kern, True)
    arrived = jnp.concatenate(arrived)
    slots = slots_of(p, pairs, table)
    current = estimate
    for iteration in range(ITERS):
        last = iteration == ITERS - 1
        mine = spread(p, slots, ids, blurred, table, arrived)
        other = lax.ppermute(mine, "view", [(0, 1), (1, 0)])
        out = update(p, count, current, mine, other, last)
        current = out[0]
        if not last:
            pieces, _ = halos(p, *out[1:])
            blurred = blur(p, ids, pieces, kern, False)[0]
    return current


def solution(mesh):
    in_specs = (
        P(("group", "gz"), "blk", None),
        P(("group", "blk", "gz", "view"), None, None, None),
        P("group", None),
        P("view", ("group", "blk", "gz"), None, None, None),
        P("group", None),
    )
    out_specs = P(("group", "gz"), "blk", None)
    return jax.shard_map(
        on_device, mesh=mesh, in_specs=in_specs, out_specs=out_specs, check_vma=False
    )
```

```python
import functools

import jax
import jax.numpy as jnp
from jax import lax
from jax.experimental import pallas as pl
from jax.experimental.pallas import tpu as pltpu
from jax.sharding import PartitionSpec as P


ITERS = 2
F32, BF16 = jnp.float32, jnp.bfloat16
VM = pl.BlockSpec(memory_space=pltpu.VMEM)
SM = pl.BlockSpec(memory_space=pltpu.SMEM)


def send_order(n_blk):
    return sorted(range(1, n_blk), key=lambda k: (k < n_blk // 2, k))


class Plan:
    def __init__(self, estimate, view_tiles, kernel_table):
        self.cz, self.ly, self.nx = estimate.shape
        self.tiles, self.ez, self.ey, _ = view_tiles.shape
        self.views_here, self.sets_here, self.taps = kernel_table.shape[:3]
        self.reach = (self.taps - 1) // 2
        self.by = self.ey - 2 * self.reach
        self.blocks = self.ly // self.by
        self.n_blk = lax.axis_size("blk")
        self.n_gz = lax.axis_size("gz")
        self.n_view = lax.axis_size("view")
        self.row_blocks = self.blocks * self.n_blk
        self.slots = -(-self.views_here * self.blocks // self.n_blk)
        self.slots = min(self.slots, self.tiles)
        self.fast = self.n_blk == 4 and self.n_gz == 2 and self.sets_here == 1
        self.n_sets = self.n_blk * self.n_gz * self.sets_here
        self.halo = 2 * self.reach
        assert self.by == 8 and self.cz == 8 and self.nx == 128 and self.taps == 7
        assert self.n_blk & (self.n_blk - 1) == 0 and self.n_blk > 1 and self.ez <= 16
        self.rows = self.ly + 16
        self.yw = 24
        self.depth = (self.taps * self.yw + 15) // 16 * 16
        self.send_order = send_order(self.n_blk)


def ranks():
    return lax.axis_index("blk"), lax.axis_index("gz"), lax.axis_index("view")


def lane_shift(plane, e, reach, lane):
    d = e - reach
    if d == 0:
        return plane
    n = plane.shape[-1]
    rolled = pltpu.roll(plane, (-d) % n, 1)
    ok = (lane < n - d) if d > 0 else (lane >= -d)
    return jnp.where(ok, rolled, jnp.zeros_like(rolled))


def sends_of(p, b, x, own_ref, sa_ref, sb_ref):
    even = b % 2 == 0
    for z in range(p.cz):
        xb = x[z].astype(BF16)
        own_ref[z] = xb
        lo, hi = xb[:8], xb[p.ly - 8 :]
        lo, hi = x[z][:8], x[z][p.ly - 8 :]
        sa_ref[z] = jnp.where(even, hi, lo).astype(BF16)
        sb_ref[z] = jnp.where(even, lo, hi).astype(BF16)


def first_kernel(p, pairs_hbm, est_hbm, tiles_hbm, table_hbm, *refs):
    own_ref, sa_ref, sb_ref, kern_ref, count_ref, *packed = refs[: 5 + p.n_blk]
    pairs_ref, blocks_ref, est_ref, tiles_ref, table_ref, sems = refs[5 + p.n_blk :]
    moves = [(est_hbm, est_ref), (table_hbm, table_ref), (pairs_hbm, pairs_ref), (pairs_hbm, blocks_ref), (tiles_hbm, tiles_ref)]
    copies = [pltpu.make_async_copy(i, j, sems.at[n]) for n, (i, j) in enumerate(moves)]
    for copy in copies:
        copy.start()
    b, g, v = ranks()
    copies[0].wait()
    sends_of(p, b, [est_ref[z] for z in range(p.cz)], own_ref, sa_ref, sb_ref)
    copies[1].wait()
    kern_ref[...] = jnp.zeros(kern_ref.shape, BF16)
    if p.sets_here == 1:
        for i in range(p.views_here):
            cube = table_ref[i, 0].astype(F32)
            rows = jnp.concatenate([cube[:, c, :] for c in range(p.taps)], axis=1)
            rows = jnp.concatenate([rows, jnp.zeros((p.taps, 128 - p.taps * p.taps), F32)], axis=1)
            rows = jnp.concatenate([rows, jnp.zeros((8 - p.taps, 128), F32)], axis=0)
            kern_ref[8 * i : 8 * i + 8, :] = rows.astype(BF16)

    copies[2].wait()
    copies[3].wait()
    for k in range(p.blocks):
        same = blocks_ref[0:1, :] == g * p.row_blocks + b * p.blocks + k
        count = jnp.sum(jnp.where(same, 1.0, 0.0), axis=1, keepdims=True)
        count_ref[8 * k : 8 * k + 8, :] = jnp.broadcast_to(count, (8, p.nx))
    copies[4].wait()
    first = ((b * p.n_gz + g) * p.n_view + v) * p.tiles
    homes = [lax.rem(pairs_ref[0, first + j], p.row_blocks) // p.blocks for j in range(p.tiles)]
    for j in range(p.tiles):
        rank = sum([(homes[i] == homes[j]).astype(jnp.int32) for i in range(j)], jnp.int32(0))
        for k in range(p.n_blk):

            @pl.when(homes[j] ^ b == k)
            def _():
                for s in range(p.ez):
                    packed[k][rank, s * p.ey : (s + 1) * p.ey, :] = tiles_ref[j, s]


def slots_kernel(p, pairs_ref, after_ref, slot_ref):
    b, g, v = ranks()
    for i in range(p.blocks * p.views_here):
        slot_ref[i] = -1

    def from_source(k, carry):
        first = (((b ^ k) * p.n_gz + g) * p.n_view + v) * p.tiles
        rank = jnp.int32(0)
        for j in range(p.tiles):
            place = lax.rem(pairs_ref[0, first + j], p.row_blocks)
            mine = place // p.blocks == b
            at = lax.rem(place, p.blocks) * p.views_here + pairs_ref[1, first + j] - v * p.views_here
            slot_ref[jnp.where(mine, at, p.blocks * p.views_here)] = k * p.slots + rank
            rank = rank + mine.astype(jnp.int32)
        return carry

    lax.fori_loop(0, p.n_blk, from_source, 0)


def slots_of(p, pairs, after):
    return pl.pallas_call(
        functools.partial(slots_kernel, p),
        out_shape=jax.ShapeDtypeStruct((p.blocks * p.views_here + 1,), jnp.int32),
        in_specs=[SM, pl.BlockSpec(memory_space=pl.ANY)], out_specs=SM, name="slots",
        compiler_params=pltpu.CompilerParams(vmem_limit_bytes=1 << 20),
    )(pairs, after)


def update_kernel(p, count_ref, est_ref, mine_ref, other_ref, new_ref, own_ref=None, sa_ref=None, sb_ref=None):
    b, _, _ = ranks()
    x = []
    for z in range(p.cz):
        rows = []
        for k in range(p.blocks):
            at = slice(k * 8, k * 8 + 8)
            total = mine_ref[z, at, :] + other_ref[z, at, :]
            rows.append(est_ref[z, at, :] * total / count_ref[at, :])
        x.append(jnp.concatenate(rows, axis=0))
        new_ref[z] = x[z]
    if own_ref is not None:
        sends_of(p, b, x, own_ref, sa_ref, sb_ref)


def sends_shape(p):
    return [
        jax.ShapeDtypeStruct((p.cz, p.ly, p.nx), BF16),
        jax.ShapeDtypeStruct((p.cz, 8, p.nx), BF16),
        jax.ShapeDtypeStruct((p.cz, 8, p.nx), BF16),
    ]


def first_sends(p, pairs, est, tiles, table):
    shapes = sends_shape(p) + [
        jax.ShapeDtypeStruct((8 * p.views_here, 128), BF16),
        jax.ShapeDtypeStruct((8 * p.blocks, p.nx), F32),
    ]
    shapes += [jax.ShapeDtypeStruct((p.slots, p.ez * p.ey, p.nx), tiles.dtype)] * p.n_blk
    return pl.pallas_call(
        functools.partial(first_kernel, p), out_shape=shapes,
        in_specs=[pl.BlockSpec(memory_space=pltpu.HBM)] * 4,
        out_specs=[VM] * len(shapes), name="first",
        scratch_shapes=[
            pltpu.SMEM(pairs.shape, pairs.dtype), pltpu.VMEM(pairs.shape, pairs.dtype), pltpu.VMEM(est.shape, est.dtype),
            pltpu.VMEM(tiles.shape, tiles.dtype), pltpu.VMEM(table.shape, table.dtype), pltpu.SemaphoreType.DMA((5,)),
        ],
        compiler_params=pltpu.CompilerParams(vmem_limit_bytes=4 << 20),
    )(*[pltpu.with_memory_space_constraint(x, pltpu.HBM) for x in (pairs, est, tiles, table)])


def update(p, count, est, mine, other, last):
    shapes = [jax.ShapeDtypeStruct(est.shape, F32)] + ([] if last else sends_shape(p))
    return pl.pallas_call(
        functools.partial(update_kernel, p), out_shape=shapes, in_specs=[VM] * 4,
        out_specs=[VM] * len(shapes), name="update", compiler_params=pltpu.CompilerParams(vmem_limit_bytes=4 << 20),
    )(count, est, mine, other)


def edges_kernel(p, own_ref, ra_ref, rb_ref, lo_ref, hi_ref=None):
    b, g, _ = ranks()
    even = b % 2 == 0
    has_lo, has_hi = b > 0, b < p.n_blk - 1

    def planes(out_ref, start):
        for i in range(p.halo):
            ra, rb = ra_ref[start + i].astype(F32), rb_ref[start + i].astype(F32)
            left = jnp.where(has_lo, jnp.where(even, rb, ra), 0.0)
            right = jnp.where(has_hi, jnp.where(even, ra, rb), 0.0)
            out_ref[i, :8] = left.astype(BF16)
            out_ref[i, 8 : 8 + p.ly] = own_ref[start + i]
            out_ref[i, 8 + p.ly :] = right.astype(BF16)

    if hi_ref is None:
        planes(lo_ref, jnp.where(g == 0, p.cz - p.halo, 0))
    else:
        planes(lo_ref, p.cz - p.halo)
        planes(hi_ref, 0)


def pairs_of(n):
    pair = [(i, i ^ 1) for i in range(n)]
    odd = [(i, (i + 1) % n if i % 2 else (i - 1) % n) for i in range(n)]
    return pair, odd


def halos(p, own, sa, sb, kern=None):
    pair, odd = pairs_of(p.n_blk)
    nz = p.cz * 8
    carry = kern is not None and p.fast
    if carry:
        a = lax.ppermute(jnp.concatenate([sa.reshape(nz, p.nx), kern]), "blk", pair)
        b = lax.ppermute(jnp.concatenate([sb.reshape(nz, p.nx), kern]), "blk", odd)
        c = lax.ppermute(kern, "blk", [(i, i ^ 2) for i in range(p.n_blk)])
        ra, rb = a[:nz].reshape(sa.shape), b[:nz].reshape(sb.shape)
        kern = jnp.concatenate([kern, a[nz:], b[nz:], c])
    else:
        ra, rb = lax.ppermute(sa, "blk", pair), lax.ppermute(sb, "blk", odd)
    two = p.n_gz == 2
    edge = jax.ShapeDtypeStruct((p.halo, p.rows, p.nx), BF16)
    out = pl.pallas_call(
        functools.partial(edges_kernel, p), out_shape=[edge] if two else [edge, edge],
        in_specs=[VM] * 3, out_specs=[VM] * (1 if two else 2), name="edges",
        compiler_params=pltpu.CompilerParams(vmem_limit_bytes=4 << 20),
    )(own, ra, rb)
    if two:
        swap = [(0, 1), (1, 0)]
        if carry:
            ne = p.halo * p.rows
            got = lax.ppermute(jnp.concatenate([out[0].reshape(ne, p.nx), kern]), "gz", swap)
            below = above = got[:ne].reshape(edge.shape)
            kern = jnp.concatenate([kern, got[ne:]])
        else:
            below = above = lax.ppermute(out[0], "gz", swap)
    else:
        ups = [(i, i + 1) for i in range(p.n_gz - 1)]
        below = lax.ppermute(out[0], "gz", ups)
        above = lax.ppermute(out[1], "gz", [(j, i) for i, j in ups])
    return (own, ra, rb, below, above), kern


def put_shifts(p, xs_ref, at, plane, lane):
    taps, yw = p.taps, p.yw
    moved = [lane_shift(plane, e, p.reach, lane) for e in range(taps)]
    for bl in range(p.blocks):
        rows = slice(8 * bl, 8 * bl + yw)
        for e in range(0, taps, 2):
            high = moved[e + 1][rows] if e + 1 < taps else jnp.zeros((p.depth - e * yw - yw, p.nx), F32)
            both = jnp.concatenate([moved[e][rows], high], axis=0).astype(BF16)
            xs_ref[bl, at, e * yw : e * yw + both.shape[0], :] = both


def put_blur(p, wf, xs_ref, bl, planes, done):
    m, nx = 16 * p.views_here, p.nx
    acc = {}
    for n, z0 in enumerate(planes):
        lo, hi = max(0, z0 - p.ez + 1), min(p.taps - 1, z0 + 1)
        both = jnp.concatenate([xs_ref[bl, 2 * n], xs_ref[bl, 2 * n + 1]], axis=1)
        got = jnp.dot(wf[m * lo : m * (hi + 1)], both, preferred_element_type=F32)
        for half in range(2):
            z = z0 + half
            for a in range(lo, hi + 1):
                s = z - a
                if 0 <= s < p.ez:
                    part = got[m * (a - lo) : m * (a - lo + 1), half * nx : (half + 1) * nx]
                    acc[s] = part if s not in acc else acc[s] + part
            for s in [s for s in acc if s + p.taps - 1 <= z or z == planes[-1] + 1]:
                done(s, acc.pop(s))


def blur_kernel(p, ids_ref, own_ref, ra_ref, rb_ref, kern_ref, *rest):
    first = len(rest) == 5
    out_ref, wf_ref, kb_ref, xs_ref, kf_ref = rest if first else (*rest[:2], None, *rest[2:])
    taps, nx, yw = p.taps, p.nx, p.yw
    row = lax.broadcasted_iota(jnp.int32, (128, 256), 0)
    col = lax.broadcasted_iota(jnp.int32, (128, 256), 1)
    select = ((row // taps == col % yw) & (row % taps == col // yw) & (row < taps * taps)).astype(BF16)
    kf_ref[...] = jnp.dot(kern_ref[...], select, preferred_element_type=F32)
    if first:
        row = lax.broadcasted_iota(jnp.int32, (128, 128), 0)
        col = lax.broadcasted_iota(jnp.int32, (128, 128), 1)
        for e in range(taps):
            select = (row // taps == taps - 1 - col % 16) & (row % taps == taps - 1 - e)
            select = (select & (row < taps * taps)).astype(BF16)
            kb_ref[e] = jnp.dot(kern_ref[...], select, preferred_element_type=F32)

    b, _, _ = ranks()
    even = b % 2 == 0
    has_left, has_right = b > 0, b < p.n_blk - 1
    lane = lax.broadcasted_iota(jnp.int32, (p.rows, nx), 1)
    for i in range(p.cz):
        ra, rb = ra_ref[i].astype(F32), rb_ref[i].astype(F32)
        left = jnp.where(has_left, jnp.where(even, rb, ra), 0.0)
        right = jnp.where(has_right, jnp.where(even, ra, rb), 0.0)
        put_shifts(p, xs_ref, i, jnp.concatenate([left, own_ref[i].astype(F32), right], axis=0), lane)

    for bl in range(p.blocks):
        wf = [[] for _ in range(taps)]
        for view in range(p.views_here):
            base = pltpu.roll(kf_ref[kernel_rows(p, ids_ref, bl, view), :], 2, 1)
            for a in range(taps):
                wide = jnp.broadcast_to(base[a : a + 1], (16, 256))
                wf[a].append(pltpu.roll(wide, 0, 1, stride=1, stride_axis=0))
        wf = jnp.concatenate([x for y in wf for x in y], axis=0).astype(BF16)[:, : p.depth]
        wf_ref[bl] = wf

        def done(s, total):
            for view in range(p.views_here):
                out_ref[bl * p.views_here + view, s] = total[16 * view : 16 * view + 16]

        put_blur(p, wf, xs_ref, bl, range(p.halo, p.halo + p.cz, 2), done)


def beside_kernel(p, below_ref, above_ref, before_ref, wf_ref, out_ref, xs_ref):
    _, g, _ = ranks()
    lane = lax.broadcasted_iota(jnp.int32, (p.rows, p.nx), 1)
    for there, ref, z0 in ((g > 0, below_ref, 0), (g < p.n_gz - 1, above_ref, p.halo + p.cz)):

        @pl.when(there)
        def _():
            for z in range(p.halo):
                put_shifts(p, xs_ref, z, ref[z].astype(F32), lane)
            for bl in range(p.blocks):

                def done(s, total):
                    for view in range(p.views_here):
                        at = bl * p.views_here + view
                        out_ref[at, s] = before_ref[at, s] + total[16 * view : 16 * view + 16]

                put_blur(p, wf_ref[bl], xs_ref, bl, range(z0, z0 + p.halo, 2), done)


def kernel_rows(p, ids_ref, bl, view):
    b, g, v = ranks()
    number = g * p.row_blocks + b * p.blocks + bl
    kid = ids_ref[v * p.views_here + view, number]
    if p.fast:
        x = (kid // p.n_gz) ^ b
        at = jnp.where(lax.rem(kid, p.n_gz) == g, 0, p.n_blk) + (x ^ (x >> 1))
        at = at * p.views_here + view
    else:
        at = view * p.n_sets + kid
    return pl.ds(pl.multiple_of(at * 8, 8), 8)


def blur(p, ids, pieces, kern, first):
    own, ra, rb, below, above = pieces
    partial = jax.ShapeDtypeStruct((p.blocks * p.views_here, p.ez, 16, p.nx), F32)
    left = jax.ShapeDtypeStruct((p.blocks, 16 * p.views_here * p.taps, p.depth), BF16)
    table = jax.ShapeDtypeStruct((p.taps, kern.shape[0], 128), F32)
    shapes = [partial, left] + ([table] if first else [])
    out = pl.pallas_call(
        functools.partial(blur_kernel, p),
        out_shape=shapes, in_specs=[SM] + [VM] * 4, out_specs=[VM] * len(shapes),
        scratch_shapes=[
            pltpu.VMEM((p.blocks, p.cz, p.depth, p.nx), BF16),
            pltpu.VMEM((kern.shape[0], 256), F32),
        ],
        name="blur", compiler_params=pltpu.CompilerParams(vmem_limit_bytes=10 << 20),
    )(ids, own, ra, rb, kern)
    whole = pl.pallas_call(
        functools.partial(beside_kernel, p),
        out_shape=partial, in_specs=[VM] * 4, out_specs=VM, input_output_aliases={2: 0},
        scratch_shapes=[pltpu.VMEM((p.blocks, p.halo, p.depth, p.nx), BF16)],
        name="beside", compiler_params=pltpu.CompilerParams(vmem_limit_bytes=10 << 20),
    )(below, above, out[0], out[1])
    return whole, out[2] if first else None


def spread_kernel(p, slot_ref, ids_ref, blur_ref, kb_ref, tiles_ref, out_ref, r_ref):
    b, g, _ = ranks()
    taps, reach, nx, views = p.taps, p.reach, p.nx, p.views_here
    has_below, has_above = g > 0, g < p.n_gz - 1
    z_low = jnp.where(has_below, 0, reach)
    z_high = jnp.where(has_above, p.ez, p.ez - reach)
    u_row = lax.broadcasted_iota(jnp.int32, (16, nx), 0)
    lane8 = lax.broadcasted_iota(jnp.int32, (8, nx), 1)

    def block(bl, carry):
        wb = [[] for _ in range(taps)]
        at = [kernel_rows(p, ids_ref, bl, view) for view in range(views)]
        for e in range(taps):
            base = kb_ref[e, at[-1], :]
            for view in range(views - 2, -1, -1):
                base = jnp.where(lane8 < 16 * view + 16, kb_ref[e, at[view], :], base)
            for a in range(taps):
                wide = jnp.broadcast_to(base[a : a + 1], (8, 128))
                wb[a].append(pltpu.roll(wide, 0, 1, stride=1, stride_axis=0))
        wb = jnp.concatenate([x for y in wb for x in y], axis=0).astype(BF16)[:, : 16 * views]
        m = 8 * taps
        y_first = (b * p.blocks + bl) * p.by - reach
        y_ok = (u_row < p.ey) & (u_row + y_first >= 0) & (u_row + y_first < p.row_blocks * p.by)
        slots = [slot_ref[bl * views + view] for view in range(views)]
        acc = {}
        for pair in range(p.ez // 2):
            s0 = pair * 2
            for s in (s0, s0 + 1):
                z_ok = (s >= z_low) & (s < z_high)
                for view in range(views):
                    tile = tiles_ref[jnp.maximum(slots[view], 0), s * p.ey : (s + 1) * p.ey, :].astype(F32)
                    tile = jnp.concatenate([tile, jnp.zeros((16 - p.ey, nx), F32)], axis=0)
                    ratio = tile / blur_ref[bl * views + view, s]
                    keep = y_ok & (z_ok & (slots[view] >= 0))
                    r_ref[bl, s, 16 * view : 16 * view + 16, :] = jnp.where(keep, ratio, 0.0).astype(BF16)
            lo, hi = max(0, 2 * reach - s0 - 1) // 2 * 2, min(taps - 1, 2 * reach + p.cz - 1 - s0)
            planes = jnp.concatenate([r_ref[bl, s0], r_ref[bl, s0 + 1]], axis=1)
            got = jnp.dot(wb[m * lo : m * (hi + 1)], planes, preferred_element_type=F32)
            for half in range(2):
                s = s0 + half
                for a in range(lo, hi + 1):
                    z = s + a - 2 * reach
                    if 0 <= z < p.cz:
                        part = got[m * (a - lo) : m * (a - lo + 1), half * nx : (half + 1) * nx]
                        acc[z] = part if z not in acc else acc[z] + part
                z = s - 2 * reach
                if 0 <= z < p.cz:
                    done = acc.pop(z)
                    term = done[8 * reach : 8 * reach + 8]
                    for e in range(taps):
                        if e != reach:
                            term = term + lane_shift(done[8 * e : 8 * e + 8], e, reach, lane8)
                    out_ref[z, bl * 8 : bl * 8 + 8, :] = term
        return carry

    for bl in range(p.blocks):
        block(bl, 0)


def spread(p, slots, ids, blurred, table, arrived):
    ins = [slots, ids, blurred, table, arrived]
    return pl.pallas_call(
        functools.partial(spread_kernel, p),
        out_shape=jax.ShapeDtypeStruct((p.cz, p.ly, p.nx), F32),
        in_specs=[SM, SM] + [VM] * (len(ins) - 2),
        out_specs=VM,
        scratch_shapes=[
            pltpu.VMEM((p.blocks, p.ez, p.views_here * 16, p.nx), BF16),
        ],
        name="spread", compiler_params=pltpu.CompilerParams(vmem_limit_bytes=6 << 20),
    )(*ins)


def on_device(estimate, view_tiles, tile_pairs, kernel_table, kernel_ids):
    p = Plan(estimate, view_tiles, kernel_table)
    pairs, ids = tile_pairs.T, kernel_ids.T
    own, sa, sb, kern, count, *packed = first_sends(p, pairs, estimate, view_tiles, kernel_table)
    pieces, gathered = halos(p, own, sa, sb, kern)
    if p.fast:
        kern = gathered
    else:
        kern = kernel_table.reshape(p.views_here, p.sets_here, p.taps, p.taps * p.taps)
        kern = jnp.pad(kern, ((0, 0), (0, 0), (0, 1), (0, 128 - p.taps * p.taps)))
        kern = kern.reshape(p.views_here, p.sets_here * 8, 128)
        kern = lax.all_gather(kern, ("blk", "gz"), axis=1, tiled=True).reshape(-1, 128)
    arrived = [packed[0]] + [None] * (p.n_blk - 1)
    for k in p.send_order:
        arrived[k] = lax.ppermute(packed[k], "blk", [(i, i ^ k) for i in range(p.n_blk)])
    blurred, table = blur(p, ids, pieces, kern, True)
    arrived = jnp.concatenate(arrived)
    slots = slots_of(p, pairs, table)
    current = estimate
    for iteration in range(ITERS):
        last = iteration == ITERS - 1
        mine = spread(p, slots, ids, blurred, table, arrived)
        other = lax.ppermute(mine, "view", [(0, 1), (1, 0)])
        out = update(p, count, current, mine, other, last)
        current = out[0]
        if not last:
            pieces, _ = halos(p, *out[1:])
            blurred = blur(p, ids, pieces, kern, False)[0]
    return current


def solution(mesh):
    in_specs = (
        P(("group", "gz"), "blk", None),
        P(("group", "blk", "gz", "view"), None, None, None),
        P("group", None),
        P("view", ("group", "blk", "gz"), None, None, None),
        P("group", None),
    )
    out_specs = P(("group", "gz"), "blk", None)
    return jax.shard_map(
        on_device, mesh=mesh, in_specs=in_specs, out_specs=out_specs, check_vma=False
    )
```

```python
import functools

import jax
import jax.numpy as jnp
from jax import lax
from jax.experimental import pallas as pl
from jax.experimental.pallas import tpu as pltpu
from jax.sharding import PartitionSpec as P


ITERS = 2
F32, BF16 = jnp.float32, jnp.bfloat16
VM = pl.BlockSpec(memory_space=pltpu.VMEM)
SM = pl.BlockSpec(memory_space=pltpu.SMEM)


def send_order(n_blk):
    return sorted(range(1, n_blk), key=lambda k: (k < n_blk // 2, k))


class Plan:
    def __init__(self, estimate, view_tiles, kernel_table):
        self.cz, self.ly, self.nx = estimate.shape
        self.tiles, self.ez, self.ey, _ = view_tiles.shape
        self.views_here, self.sets_here, self.taps = kernel_table.shape[:3]
        self.reach = (self.taps - 1) // 2
        self.by = self.ey - 2 * self.reach
        self.blocks = self.ly // self.by
        self.n_blk = lax.axis_size("blk")
        self.n_gz = lax.axis_size("gz")
        self.n_view = lax.axis_size("view")
        self.row_blocks = self.blocks * self.n_blk
        self.slots = -(-self.views_here * self.blocks // self.n_blk)
        self.slots = min(self.slots, self.tiles)
        self.fast = self.n_blk == 4 and self.n_gz == 2 and self.sets_here == 1
        self.n_sets = self.n_blk * self.n_gz * self.sets_here
        self.halo = 2 * self.reach
        assert self.by == 8 and self.cz == 8 and self.nx == 128 and self.taps == 7
        assert self.n_blk & (self.n_blk - 1) == 0 and self.n_blk > 1 and self.ez <= 16
        self.rows = self.ly + 16
        self.yw = 24
        self.depth = (self.taps * self.yw + 15) // 16 * 16
        self.send_order = send_order(self.n_blk)


def ranks():
    return lax.axis_index("blk"), lax.axis_index("gz"), lax.axis_index("view")


def lane_shift(plane, e, reach, lane):
    d = e - reach
    if d == 0:
        return plane
    n = plane.shape[-1]
    rolled = pltpu.roll(plane, (-d) % n, 1)
    ok = (lane < n - d) if d > 0 else (lane >= -d)
    return jnp.where(ok, rolled, jnp.zeros_like(rolled))


def sends_of(p, b, x, own_ref, sa_ref, sb_ref):
    even = b % 2 == 0
    for z in range(p.cz):
        xb = x[z].astype(BF16)
        own_ref[z] = xb
        lo, hi = xb[:8], xb[p.ly - 8 :]
        lo, hi = x[z][:8], x[z][p.ly - 8 :]
        sa_ref[z] = jnp.where(even, hi, lo).astype(BF16)
        sb_ref[z] = jnp.where(even, lo, hi).astype(BF16)


def first_kernel(p, pairs_hbm, est_hbm, tiles_hbm, table_hbm, *refs):
    own_ref, sa_ref, sb_ref, kern_ref, count_ref, *packed = refs[: 5 + p.n_blk]
    pairs_ref, blocks_ref, est_ref, tiles_ref, table_ref, sems = refs[5 + p.n_blk :]
    moves = [(est_hbm, est_ref), (table_hbm, table_ref), (pairs_hbm, pairs_ref), (pairs_hbm, blocks_ref), (tiles_hbm, tiles_ref)]
    copies = [pltpu.make_async_copy(i, j, sems.at[n]) for n, (i, j) in enumerate(moves)]
    for copy in copies:
        copy.start()
    b, g, v = ranks()
    copies[0].wait()
    sends_of(p, b, [est_ref[z] for z in range(p.cz)], own_ref, sa_ref, sb_ref)
    copies[1].wait()
    kern_ref[...] = jnp.zeros(kern_ref.shape, BF16)
    if p.sets_here == 1:
        for i in range(p.views_here):
            cube = table_ref[i, 0].astype(F32)
            rows = jnp.concatenate([cube[:, c, :] for c in range(p.taps)], axis=1)
            rows = jnp.concatenate([rows, jnp.zeros((p.taps, 128 - p.taps * p.taps), F32)], axis=1)
            rows = jnp.concatenate([rows, jnp.zeros((8 - p.taps, 128), F32)], axis=0)
            kern_ref[8 * i : 8 * i + 8, :] = rows.astype(BF16)

    copies[2].wait()
    copies[3].wait()
    for k in range(p.blocks):
        same = blocks_ref[0:1, :] == g * p.row_blocks + b * p.blocks + k
        count = jnp.sum(jnp.where(same, 1.0, 0.0), axis=1, keepdims=True)
        count_ref[8 * k : 8 * k + 8, :] = jnp.broadcast_to(count, (8, p.nx))
    copies[4].wait()
    first = ((b * p.n_gz + g) * p.n_view + v) * p.tiles
    homes = [lax.rem(pairs_ref[0, first + j], p.row_blocks) // p.blocks for j in range(p.tiles)]
    for j in range(p.tiles):
        rank = sum([(homes[i] == homes[j]).astype(jnp.int32) for i in range(j)], jnp.int32(0))
        for k in range(p.n_blk):

            @pl.when(homes[j] ^ b == k)
            def _():
                for s in range(p.ez):
                    packed[k][rank, s * p.ey : (s + 1) * p.ey, :] = tiles_ref[j, s]


def slots_kernel(p, pairs_ref, after_ref, slot_ref):
    b, g, v = ranks()
    for i in range(p.blocks * p.views_here):
        slot_ref[i] = -1

    def from_source(k, carry):
        first = (((b ^ k) * p.n_gz + g) * p.n_view + v) * p.tiles
        rank = jnp.int32(0)
        for j in range(p.tiles):
            place = lax.rem(pairs_ref[0, first + j], p.row_blocks)
            mine = place // p.blocks == b
            at = lax.rem(place, p.blocks) * p.views_here + pairs_ref[1, first + j] - v * p.views_here
            slot_ref[jnp.where(mine, at, p.blocks * p.views_here)] = k * p.slots + rank
            rank = rank + mine.astype(jnp.int32)
        return carry

    lax.fori_loop(0, p.n_blk, from_source, 0)


def slots_of(p, pairs, after):
    return pl.pallas_call(
        functools.partial(slots_kernel, p),
        out_shape=jax.ShapeDtypeStruct((p.blocks * p.views_here + 1,), jnp.int32),
        in_specs=[SM, pl.BlockSpec(memory_space=pl.ANY)], out_specs=SM, name="slots",
        compiler_params=pltpu.CompilerParams(vmem_limit_bytes=1 << 20),
    )(pairs, after)


def update_kernel(p, count_ref, est_ref, mine_ref, other_ref, new_ref, own_ref=None, sa_ref=None, sb_ref=None):
    b, _, _ = ranks()
    x = []
    for z in range(p.cz):
        rows = []
        for k in range(p.blocks):
            at = slice(k * 8, k * 8 + 8)
            total = mine_ref[z, at, :] + other_ref[z, at, :]
            rows.append(est_ref[z, at, :] * total / count_ref[at, :])
        x.append(jnp.concatenate(rows, axis=0))
        new_ref[z] = x[z]
    if own_ref is not None:
        sends_of(p, b, x, own_ref, sa_ref, sb_ref)


def sends_shape(p):
    return [
        jax.ShapeDtypeStruct((p.cz, p.ly, p.nx), BF16),
        jax.ShapeDtypeStruct((p.cz, 8, p.nx), BF16),
        jax.ShapeDtypeStruct((p.cz, 8, p.nx), BF16),
    ]


def first_sends(p, pairs, est, tiles, table):
    shapes = sends_shape(p) + [
        jax.ShapeDtypeStruct((8 * p.views_here, 128), BF16),
        jax.ShapeDtypeStruct((8 * p.blocks, p.nx), F32),
    ]
    shapes += [jax.ShapeDtypeStruct((p.slots, p.ez * p.ey, p.nx), tiles.dtype)] * p.n_blk
    return pl.pallas_call(
        functools.partial(first_kernel, p), out_shape=shapes,
        in_specs=[pl.BlockSpec(memory_space=pltpu.HBM)] * 4,
        out_specs=[VM] * len(shapes), name="first",
        scratch_shapes=[
            pltpu.SMEM(pairs.shape, pairs.dtype), pltpu.VMEM(pairs.shape, pairs.dtype), pltpu.VMEM(est.shape, est.dtype),
            pltpu.VMEM(tiles.shape, tiles.dtype), pltpu.VMEM(table.shape, table.dtype), pltpu.SemaphoreType.DMA((5,)),
        ],
        compiler_params=pltpu.CompilerParams(vmem_limit_bytes=4 << 20),
    )(*[pltpu.with_memory_space_constraint(x, pltpu.HBM) for x in (pairs, est, tiles, table)])


def update(p, count, est, mine, other, last):
    shapes = [jax.ShapeDtypeStruct(est.shape, F32)] + ([] if last else sends_shape(p))
    return pl.pallas_call(
        functools.partial(update_kernel, p), out_shape=shapes, in_specs=[VM] * 4,
        out_specs=[VM] * len(shapes), name="update", compiler_params=pltpu.CompilerParams(vmem_limit_bytes=4 << 20),
    )(count, est, mine, other)


def edges_kernel(p, own_ref, ra_ref, rb_ref, lo_ref, hi_ref=None):
    b, g, _ = ranks()
    even = b % 2 == 0
    has_lo, has_hi = b > 0, b < p.n_blk - 1

    def planes(out_ref, start):
        for i in range(p.halo):
            ra, rb = ra_ref[start + i].astype(F32), rb_ref[start + i].astype(F32)
            left = jnp.where(has_lo, jnp.where(even, rb, ra), 0.0)
            right = jnp.where(has_hi, jnp.where(even, ra, rb), 0.0)
            out_ref[i, :8] = left.astype(BF16)
            out_ref[i, 8 : 8 + p.ly] = own_ref[start + i]
            out_ref[i, 8 + p.ly :] = right.astype(BF16)

    if hi_ref is None:
        planes(lo_ref, jnp.where(g == 0, p.cz - p.halo, 0))
    else:
        planes(lo_ref, p.cz - p.halo)
        planes(hi_ref, 0)


def pairs_of(n):
    pair = [(i, i ^ 1) for i in range(n)]
    odd = [(i, (i + 1) % n if i % 2 else (i - 1) % n) for i in range(n)]
    return pair, odd


def halos(p, own, sa, sb, kern=None):
    pair, odd = pairs_of(p.n_blk)
    nz = p.cz * 8
    carry = kern is not None and p.fast
    if carry:
        a = lax.ppermute(jnp.concatenate([sa.reshape(nz, p.nx), kern]), "blk", pair)
        b = lax.ppermute(jnp.concatenate([sb.reshape(nz, p.nx), kern]), "blk", odd)
        c = lax.ppermute(kern, "blk", [(i, i ^ 2) for i in range(p.n_blk)])
        ra, rb = a[:nz].reshape(sa.shape), b[:nz].reshape(sb.shape)
        kern = jnp.concatenate([kern, a[nz:], b[nz:], c])
    else:
        inner = [(i, j) for i, j in odd if abs(i - j) == 1]
        ra, rb = lax.ppermute(sa, "blk", pair), lax.ppermute(sb, "blk", inner)
    two = p.n_gz == 2
    edge = jax.ShapeDtypeStruct((p.halo, p.rows, p.nx), BF16)
    out = pl.pallas_call(
        functools.partial(edges_kernel, p), out_shape=[edge] if two else [edge, edge],
        in_specs=[VM] * 3, out_specs=[VM] * (1 if two else 2), name="edges",
        compiler_params=pltpu.CompilerParams(vmem_limit_bytes=4 << 20),
    )(own, ra, rb)
    if two:
        swap = [(0, 1), (1, 0)]
        if carry:
            ne = p.halo * p.rows
            got = lax.ppermute(jnp.concatenate([out[0].reshape(ne, p.nx), kern]), "gz", swap)
            below = above = got[:ne].reshape(edge.shape)
            kern = jnp.concatenate([kern, got[ne:]])
        else:
            below = above = lax.ppermute(out[0], "gz", swap)
    else:
        ups = [(i, i + 1) for i in range(p.n_gz - 1)]
        below = lax.ppermute(out[0], "gz", ups)
        above = lax.ppermute(out[1], "gz", [(j, i) for i, j in ups])
    return (own, ra, rb, below, above), kern


def put_shifts(p, xs_ref, at, plane, lane):
    taps, yw = p.taps, p.yw
    moved = [lane_shift(plane, e, p.reach, lane) for e in range(taps)]
    for bl in range(p.blocks):
        rows = slice(8 * bl, 8 * bl + yw)
        for e in range(0, taps, 2):
            high = moved[e + 1][rows] if e + 1 < taps else jnp.zeros((p.depth - e * yw - yw, p.nx), F32)
            both = jnp.concatenate([moved[e][rows], high], axis=0).astype(BF16)
            xs_ref[bl, at, e * yw : e * yw + both.shape[0], :] = both


def put_blur(p, wf, xs_ref, bl, planes, done):
    m, nx = 16 * p.views_here, p.nx
    acc = {}
    for n, z0 in enumerate(planes):
        lo, hi = max(0, z0 - p.ez + 1), min(p.taps - 1, z0 + 1)
        both = jnp.concatenate([xs_ref[bl, 2 * n], xs_ref[bl, 2 * n + 1]], axis=1)
        got = jnp.dot(wf[m * lo : m * (hi + 1)], both, preferred_element_type=F32)
        for half in range(2):
            z = z0 + half
            for a in range(lo, hi + 1):
                s = z - a
                if 0 <= s < p.ez:
                    part = got[m * (a - lo) : m * (a - lo + 1), half * nx : (half + 1) * nx]
                    acc[s] = part if s not in acc else acc[s] + part
            for s in [s for s in acc if s + p.taps - 1 <= z or z == planes[-1] + 1]:
                done(s, acc.pop(s))


def blur_kernel(p, ids_ref, own_ref, ra_ref, rb_ref, kern_ref, *rest):
    first = len(rest) == 5
    out_ref, wf_ref, kb_ref, xs_ref, kf_ref = rest if first else (*rest[:2], None, *rest[2:])
    taps, nx, yw = p.taps, p.nx, p.yw
    row = lax.broadcasted_iota(jnp.int32, (128, 256), 0)
    col = lax.broadcasted_iota(jnp.int32, (128, 256), 1)
    select = ((row // taps == col % yw) & (row % taps == col // yw) & (row < taps * taps)).astype(BF16)
    kf_ref[...] = jnp.dot(kern_ref[...], select, preferred_element_type=F32)
    if first:
        row = lax.broadcasted_iota(jnp.int32, (128, 128), 0)
        col = lax.broadcasted_iota(jnp.int32, (128, 128), 1)
        for e in range(taps):
            select = (row // taps == taps - 1 - col % 16) & (row % taps == taps - 1 - e)
            select = (select & (row < taps * taps)).astype(BF16)
            kb_ref[e] = jnp.dot(kern_ref[...], select, preferred_element_type=F32)

    b, _, _ = ranks()
    even = b % 2 == 0
    has_left, has_right = b > 0, b < p.n_blk - 1
    lane = lax.broadcasted_iota(jnp.int32, (p.rows, nx), 1)
    for i in range(p.cz):
        ra, rb = ra_ref[i].astype(F32), rb_ref[i].astype(F32)
        left = jnp.where(has_left, jnp.where(even, rb, ra), 0.0)
        right = jnp.where(has_right, jnp.where(even, ra, rb), 0.0)
        put_shifts(p, xs_ref, i, jnp.concatenate([left, own_ref[i].astype(F32), right], axis=0), lane)

    for bl in range(p.blocks):
        wf = [[] for _ in range(taps)]
        for view in range(p.views_here):
            base = pltpu.roll(kf_ref[kernel_rows(p, ids_ref, bl, view), :], 2, 1)
            for a in range(taps):
                wide = jnp.broadcast_to(base[a : a + 1], (16, 256))
                wf[a].append(pltpu.roll(wide, 0, 1, stride=1, stride_axis=0))
        wf = jnp.concatenate([x for y in wf for x in y], axis=0).astype(BF16)[:, : p.depth]
        wf_ref[bl] = wf

        def done(s, total):
            for view in range(p.views_here):
                out_ref[bl * p.views_here + view, s] = total[16 * view : 16 * view + 16]

        put_blur(p, wf, xs_ref, bl, range(p.halo, p.halo + p.cz, 2), done)


def beside_kernel(p, below_ref, above_ref, before_ref, wf_ref, out_ref, xs_ref):
    _, g, _ = ranks()
    lane = lax.broadcasted_iota(jnp.int32, (p.rows, p.nx), 1)
    for there, ref, z0 in ((g > 0, below_ref, 0), (g < p.n_gz - 1, above_ref, p.halo + p.cz)):

        @pl.when(there)
        def _():
            for z in range(p.halo):
                put_shifts(p, xs_ref, z, ref[z].astype(F32), lane)
            for bl in range(p.blocks):

                def done(s, total):
                    for view in range(p.views_here):
                        at = bl * p.views_here + view
                        out_ref[at, s] = before_ref[at, s] + total[16 * view : 16 * view + 16]

                put_blur(p, wf_ref[bl], xs_ref, bl, range(z0, z0 + p.halo, 2), done)


def kernel_rows(p, ids_ref, bl, view):
    b, g, v = ranks()
    number = g * p.row_blocks + b * p.blocks + bl
    kid = ids_ref[v * p.views_here + view, number]
    if p.fast:
        x = (kid // p.n_gz) ^ b
        at = jnp.where(lax.rem(kid, p.n_gz) == g, 0, p.n_blk) + (x ^ (x >> 1))
        at = at * p.views_here + view
    else:
        at = view * p.n_sets + kid
    return pl.ds(pl.multiple_of(at * 8, 8), 8)


def blur(p, ids, pieces, kern, first):
    own, ra, rb, below, above = pieces
    partial = jax.ShapeDtypeStruct((p.blocks * p.views_here, p.ez, 16, p.nx), F32)
    left = jax.ShapeDtypeStruct((p.blocks, 16 * p.views_here * p.taps, p.depth), BF16)
    table = jax.ShapeDtypeStruct((p.taps, kern.shape[0], 128), F32)
    shapes = [partial, left] + ([table] if first else [])
    out = pl.pallas_call(
        functools.partial(blur_kernel, p),
        out_shape=shapes, in_specs=[SM] + [VM] * 4, out_specs=[VM] * len(shapes),
        scratch_shapes=[
            pltpu.VMEM((p.blocks, p.cz, p.depth, p.nx), BF16),
            pltpu.VMEM((kern.shape[0], 256), F32),
        ],
        name="blur", compiler_params=pltpu.CompilerParams(vmem_limit_bytes=10 << 20),
    )(ids, own, ra, rb, kern)
    whole = pl.pallas_call(
        functools.partial(beside_kernel, p),
        out_shape=partial, in_specs=[VM] * 4, out_specs=VM, input_output_aliases={2: 0},
        scratch_shapes=[pltpu.VMEM((p.blocks, p.halo, p.depth, p.nx), BF16)],
        name="beside", compiler_params=pltpu.CompilerParams(vmem_limit_bytes=10 << 20),
    )(below, above, out[0], out[1])
    return whole, out[2] if first else None


def spread_kernel(p, slot_ref, ids_ref, blur_ref, kb_ref, tiles_ref, out_ref, r_ref):
    b, g, _ = ranks()
    taps, reach, nx, views = p.taps, p.reach, p.nx, p.views_here
    has_below, has_above = g > 0, g < p.n_gz - 1
    z_low = jnp.where(has_below, 0, reach)
    z_high = jnp.where(has_above, p.ez, p.ez - reach)
    u_row = lax.broadcasted_iota(jnp.int32, (16, nx), 0)
    lane8 = lax.broadcasted_iota(jnp.int32, (8, nx), 1)

    pitch = 16 * views
    depth = pitch * taps

    def block(bl):
        wb = []
        at = [kernel_rows(p, ids_ref, bl, view) for view in range(views)]
        for e in range(taps):
            base = jnp.where(lane8 < pitch, kb_ref[e, at[-1], :], 0.0)
            for view in range(views - 2, -1, -1):
                base = jnp.where(lane8 < 16 * view + 16, kb_ref[e, at[view], :], base)
            wide = [jnp.zeros((8, 128), F32)] * (-(-depth // 128))
            for a in range(taps):
                begin = pitch * (taps - 1 - a)
                n, off = begin // 128, begin % 128
                part = jnp.broadcast_to(base[a : a + 1], (8, 128))
                part = pltpu.roll(part, off, 1, stride=1, stride_axis=0)
                if off + pitch <= 128:
                    wide[n] = wide[n] + part
                else:
                    wide[n] = wide[n] + jnp.where(lane8 >= off, part, 0.0)
                    wide[n + 1] = wide[n + 1] + jnp.where(lane8 < off, part, 0.0)
            wb.append(jnp.concatenate(wide, axis=1))
        wb = jnp.concatenate(wb, axis=0).astype(BF16)[:, :depth]
        y_first = (b * p.blocks + bl) * p.by - reach
        y_ok = (u_row < p.ey) & (u_row + y_first >= 0) & (u_row + y_first < p.row_blocks * p.by)
        slots = [slot_ref[bl * views + view] for view in range(views)]
        ready = 0
        for z0 in range(0, p.cz, 2):
            for s in range(ready, z0 + taps + 1):
                z_ok = (s >= z_low) & (s < z_high)
                for view in range(views):
                    tile = tiles_ref[jnp.maximum(slots[view], 0), s * p.ey : (s + 1) * p.ey, :].astype(F32)
                    tile = jnp.concatenate([tile, jnp.zeros((16 - p.ey, nx), F32)], axis=0)
                    ratio = tile / blur_ref[bl * views + view, s]
                    keep = y_ok & (z_ok & (slots[view] >= 0))
                    r_ref[bl, s, 16 * view : 16 * view + 16, :] = jnp.where(keep, ratio, 0.0).astype(BF16)
            ready = z0 + taps + 1
            planes = [r_ref[bl, z : z + taps].reshape(depth, nx) for z in (z0, z0 + 1)]
            got = jnp.dot(wb, jnp.concatenate(planes, axis=1), preferred_element_type=F32)
            for half in range(2):
                done = got[:, half * nx : (half + 1) * nx]
                term = done[8 * reach : 8 * reach + 8]
                for e in range(taps):
                    if e != reach:
                        term = term + lane_shift(done[8 * e : 8 * e + 8], e, reach, lane8)
                out_ref[z0 + half, bl * 8 : bl * 8 + 8, :] = term

    for bl in range(p.blocks):
        block(bl)


def spread(p, slots, ids, blurred, table, arrived):
    ins = [slots, ids, blurred, table, arrived]
    return pl.pallas_call(
        functools.partial(spread_kernel, p),
        out_shape=jax.ShapeDtypeStruct((p.cz, p.ly, p.nx), F32),
        in_specs=[SM, SM] + [VM] * (len(ins) - 2),
        out_specs=VM,
        scratch_shapes=[
            pltpu.VMEM((p.blocks, p.ez, p.views_here * 16, p.nx), BF16),
        ],
        name="spread", compiler_params=pltpu.CompilerParams(vmem_limit_bytes=6 << 20),
    )(*ins)


def on_device(estimate, view_tiles, tile_pairs, kernel_table, kernel_ids):
    p = Plan(estimate, view_tiles, kernel_table)
    pairs, ids = tile_pairs.T, kernel_ids.T
    own, sa, sb, kern, count, *packed = first_sends(p, pairs, estimate, view_tiles, kernel_table)
    pieces, gathered = halos(p, own, sa, sb, kern)
    if p.fast:
        kern = gathered
    else:
        kern = kernel_table.reshape(p.views_here, p.sets_here, p.taps, p.taps * p.taps)
        kern = jnp.pad(kern, ((0, 0), (0, 0), (0, 1), (0, 128 - p.taps * p.taps)))
        kern = kern.reshape(p.views_here, p.sets_here * 8, 128)
        kern = lax.all_gather(kern, ("blk", "gz"), axis=1, tiled=True).reshape(-1, 128)
    arrived = [packed[0]] + [None] * (p.n_blk - 1)
    for k in p.send_order:
        arrived[k] = lax.ppermute(packed[k], "blk", [(i, i ^ k) for i in range(p.n_blk)])
    blurred, table = blur(p, ids, pieces, kern, True)
    arrived = jnp.concatenate(arrived)
    slots = slots_of(p, pairs, table)
    current = estimate
    for iteration in range(ITERS):
        last = iteration == ITERS - 1
        mine = spread(p, slots, ids, blurred, table, arrived)
        other = lax.ppermute(mine, "view", [(0, 1), (1, 0)])
        out = update(p, count, current, mine, other, last)
        current = out[0]
        if not last:
            pieces, _ = halos(p, *out[1:])
            blurred = blur(p, ids, pieces, kern, False)[0]
    return current


def solution(mesh):
    in_specs = (
        P(("group", "gz"), "blk", None),
        P(("group", "blk", "gz", "view"), None, None, None),
        P("group", None),
        P("view", ("group", "blk", "gz"), None, None, None),
        P("group", None),
    )
    out_specs = P(("group", "gz"), "blk", None)
    return jax.shard_map(
        on_device, mesh=mesh, in_specs=in_specs, out_specs=out_specs, check_vma=False
    )
```
